32 devices in a mesh: groups: 2 (over x), dp: 16 (over z, y, core).
Axes of the slice: x: 2, y: 2, z: 4, core: 2. Of those that a mesh axis runs over, the one named last changes fastest.
Arguments:
- states: bfloat16 [16384, 1024], P(('groups', 'dp')), parts along dimension 0, may hold values from -6 to 6
- lengths: int32 [64], P(('groups', 'dp')), parts along dimension 0, may hold values from 1 to 256, as said below
- norm_gain: bfloat16 [1024], replicated, may hold values from 0.5 to 2
- w_gate: bfloat16 [1024, 1536], replicated, may hold values from -0.1875 to 0.1875
- w_up: bfloat16 [1024, 1536], replicated, may hold values from -0.1875 to 0.1875
- w_down: bfloat16 [1536, 1024], replicated, may hold values from -0.15625 to 0.15625
- context: bfloat16 [64, 4096], P('groups', 'dp'), parts along dimension 0, may hold values from -6 to 6
- w_out: bfloat16 [4096, 4096], P('dp'), may hold values from -0.09375 to 0.09375
- resid_stream: bfloat16 [64, 4096], P('groups'), parts along dimension 0, may hold values from -6 to 6
- teacher_gain: bfloat16 [4096], replicated, may hold values from 0.5 to 2
Outputs:
- gram_loss: float32 [2], P('groups'), parts along dimension 0
- grad_gate: float32 [2048, 1536], P(('groups', 'dp')), parts along dimension 0
- grad_up: float32 [2048, 1536], P(('groups', 'dp')), parts along dimension 0
- grad_down: float32 [3072, 1024], P(('groups', 'dp')), parts along dimension 0
The draws below stay inside these ranges and needn't reach their ends.
There are 2 independent parts, one for each index of `groups`. The reference program is written for one: setup_inputs(seed, part) draws one part's arguments, and reference() takes and returns one part's arrays. A program takes and returns all parts, laid end to end along the dimension named above; an argument that names none is the same for every part. Nothing has to cross between parts.
Inputs may be any that keep to these rules, and one draw needn't show every extreme that they name: `lengths`: some document of every group fills all 256 slots and some has a single valid token.
All inputs are finite; a program needn't handle non-finite values.
Results may differ from the reference program's by a relative error of at most 0.004.
Values may be sent and summed in bfloat16 or wider, within the bound.
A program may use at most 128 MiB of HBM per device.

```python
import math
import jax
import jax.numpy as jnp
from jax import lax

SD = 1024
FF = 1536
TD = 4096
SEQ = 256
DOCS = 32
TOKENS = 8192


def draw_lengths(key, part):
    drawn_lengths = jax.random.randint(key, (DOCS,), 1, SEQ + 1)
    full_index = jax.random.randint(jax.random.fold_in(key, 7), (), 0, DOCS)
    positions = jnp.arange(DOCS, dtype=jnp.int32)
    drawn_lengths = jnp.where(positions == full_index, SEQ, drawn_lengths)
    drawn_lengths = jnp.where(positions == (full_index + 1) % DOCS, 1, drawn_lengths)
    return drawn_lengths.astype(jnp.int32)


def steps_of(key, extent, shards, low, largest):
    def one(axis_at, shards_of):
        steps = jax.random.uniform(jax.random.fold_in(jax.random.fold_in(key, 6), axis_at), (shards_of,), jnp.float32, low / len(shards), largest / len(shards))
        return jnp.repeat(jnp.exp(steps), extent[axis_at] // shards_of).reshape((-1,) + (1,) * (len(extent) - axis_at - 1))

    factor_of = one(*shards[0])
    for cut in shards[1:]:
        factor_of = factor_of * one(*cut)
    return factor_of


def scatter_about(rng, extent, deviation, limit, cuts=(), held_as=jnp.bfloat16):
    entries = jax.random.normal(rng, extent, jnp.float32) * deviation
    if len(cuts) > 0:
        entries = steps_of(rng, extent, cuts, -0.22, 0.18) * entries
    return jnp.clip(entries, min=-limit, max=limit).astype(held_as)


def setup_inputs(seed: int = 0, part: int = 0) -> dict:
    splits = jax.random.split(jax.random.key(seed), 11)
    own_keys = jax.random.split(jax.random.fold_in(splits[10], part), 11)
    states = scatter_about(own_keys[0], (TOKENS, SD), 1.0, 6.0, ((0, 16),))
    lengths = draw_lengths(jax.random.fold_in(jax.random.fold_in(splits[10], part), 71), part)
    norm_gain = jnp.clip(jnp.exp(jax.random.uniform(splits[2], (SD,), jnp.float32, math.log(0.5), math.log(2.0))), 0.5, 2.0).astype(jnp.bfloat16)
    w_gate = scatter_about(splits[3], (SD, FF), SD ** -0.5, 0.1875)
    w_up = scatter_about(splits[4], (SD, FF), SD ** -0.5, 0.1875)
    w_down = scatter_about(splits[5], (FF, SD), FF ** -0.5, 0.15625)
    context = scatter_about(own_keys[6], (DOCS, TD), 1.0, 6.0, ((1, 16),))
    w_out = scatter_about(splits[7], (TD, TD), TD ** -0.5, 0.09375, ((0, 16),))
    resid_stream = scatter_about(own_keys[8], (DOCS, TD), 1.0, 6.0)
    teacher_gain = jnp.clip(jnp.exp(jax.random.uniform(splits[9], (TD,), jnp.float32, math.log(0.5), math.log(2.0))), 0.5, 2.0).astype(jnp.bfloat16)
    return dict(states=states, lengths=lengths, norm_gain=norm_gain, w_gate=w_gate, w_up=w_up, w_down=w_down, context=context, w_out=w_out, resid_stream=resid_stream, teacher_gain=teacher_gain)


EPS = 1e-06
LOSS_SCALE = 4096.0

def teacher_embed(attn_rows, resid_rows, teacher_gain):
    scaled_rows = teacher_gain.astype(jnp.float32) * (resid_rows.astype(jnp.float32) + attn_rows)
    inv_teacher = lax.rsqrt(lax.optimization_barrier(jnp.sum(scaled_rows * scaled_rows, axis=1, keepdims=True)) + EPS)
    return (scaled_rows * inv_teacher).astype(jnp.bfloat16)

def reference(states, lengths, norm_gain, w_gate, w_up, w_down, context, w_out, resid_stream, teacher_gain):
    attn_rows = jnp.dot(context, w_out, preferred_element_type=jnp.float32)
    teacher_rows = teacher_embed(attn_rows, resid_stream, teacher_gain)
    gram_teacher = jnp.dot(teacher_rows, teacher_rows.T, preferred_element_type=jnp.float32)
    states_wide = states.astype(jnp.float32)
    inv_rms = lax.rsqrt(lax.optimization_barrier(jnp.mean(states_wide * states_wide, axis=1, keepdims=True)) + EPS)
    normed = (states_wide * inv_rms * norm_gain.astype(jnp.float32)).astype(jnp.bfloat16)
    gate_pre = jnp.dot(normed, w_gate, preferred_element_type=jnp.float32)
    up_pre = jnp.dot(normed, w_up, preferred_element_type=jnp.float32)
    hidden = (jax.nn.silu(gate_pre) * up_pre).astype(jnp.bfloat16)
    layer_out = states_wide + jnp.dot(hidden, w_down, preferred_element_type=jnp.float32)
    positions = jnp.arange(SEQ, dtype=jnp.int32)
    valid_mask = (positions[None, :] < lengths[:, None]).astype(jnp.float32)
    counts = lengths.astype(jnp.float32)
    pooled = lax.optimization_barrier(jnp.sum(layer_out.reshape(DOCS, SEQ, SD) * valid_mask[:, :, None], axis=1)) / counts[:, None]
    inv_norm = lax.rsqrt(lax.optimization_barrier(jnp.sum(pooled * pooled, axis=1, keepdims=True)) + EPS)
    unit_rows = pooled * inv_norm
    embed_rows = unit_rows.astype(jnp.bfloat16)
    gram_student = jnp.dot(embed_rows, embed_rows.T, preferred_element_type=jnp.float32)
    gram_diff = gram_student - gram_teacher
    diff_norm = jnp.sqrt(jnp.sum(gram_diff * gram_diff) + EPS)
    teacher_norm = jnp.sqrt(jnp.sum(gram_teacher * gram_teacher))
    gram_loss = diff_norm / teacher_norm
    d_gram = LOSS_SCALE * gram_diff / (diff_norm * teacher_norm)
    d_embed = 2.0 * jnp.dot(d_gram, embed_rows.astype(jnp.float32), precision=lax.Precision.HIGHEST)
    along = lax.optimization_barrier(jnp.sum(unit_rows * d_embed, axis=1, keepdims=True))
    d_pooled = (d_embed - unit_rows * along) * inv_norm
    d_doc = (d_pooled / counts[:, None]).astype(jnp.bfloat16)
    d_token = (d_doc.astype(jnp.float32)[:, None, :] * valid_mask[:, :, None]).astype(jnp.bfloat16).reshape(TOKENS, SD)
    grad_down = jnp.dot(hidden.T, d_token, preferred_element_type=jnp.float32)
    d_hidden = jnp.dot(d_doc, w_down.T, preferred_element_type=jnp.float32)
    d_hidden_tok = (d_hidden[:, None, :] * valid_mask[:, :, None]).reshape(TOKENS, FF)
    sigmoid_gate = jax.nn.sigmoid(gate_pre)
    d_gate = (d_hidden_tok * up_pre * sigmoid_gate * (1.0 + gate_pre * (1.0 - sigmoid_gate))).astype(jnp.bfloat16)
    d_up = (d_hidden_tok * jax.nn.silu(gate_pre)).astype(jnp.bfloat16)
    grad_gate = jnp.dot(normed.T, d_gate, preferred_element_type=jnp.float32)
    grad_up = jnp.dot(normed.T, d_up, preferred_element_type=jnp.float32)
    return (gram_loss.reshape(1), grad_gate, grad_up, grad_down)
```

```python
import functools

import jax
import jax.numpy as jnp
from jax import lax
from jax.experimental import pallas as pl
from jax.experimental.pallas import tpu as pltpu
from jax.sharding import PartitionSpec as P

EPS = 1e-06
LOSS_SCALE = 4096.0
MESH = pl.DeviceIdType.MESH
F32 = jnp.float32
BF16 = jnp.bfloat16


def rows_product(left_rows, right_rows):
    return lax.dot_general(
        left_rows, right_rows, (((1,), (1,)), ((), ())), preferred_element_type=F32
    )


def split3(wide):
    high = wide.astype(BF16)
    rest = wide - high.astype(F32)
    middle = rest.astype(BF16)
    low = (rest - middle.astype(F32)).astype(BF16)
    return high, middle, low


def step_kernel(
    n, width, nz, nd,
    states_in, lengths, norm_gain, w_gate_in, w_up_in, w_down_in, context_in, w_out_in, resid_in, gain,
    loss_out, wide_out, down_out,
    states, w_gate, w_up, w_down, context, w_out, resid,
    t_send, t_recv, g_all, p_all, h_own, h_send, h_recv, s_own, big, big_h, feats, feats_in, acts, d_hid,
    y_send, y_part, y_recv, n_send, n_recv, z_send, z_recv, z_part, d_send, d_recv,
    zn_send, zn_recv, zn_part, zz_send, zz_recv, zz_part, zy_send, zy_recv,
    in_sem, wide_sem, all_ssem, all_rsem, feats_sem, ssem, acts_rsem,
    y_rsem, n_rsem, z_rsem, d_rsem, zn_rsem, zz_rsem, zy_rsem,
):
    me = lax.axis_index("dp")
    core = lax.rem(me, 2)
    row = lax.rem(lax.div(me, 2), 2)
    col = lax.div(me, 4)
    parity = lax.rem(col, 2)
    half = lax.div(col, 2)
    cols = n // 4
    halves = cols // 2
    lane = row * 2 + core
    sibling = me + 1 - 2 * core
    across = me + 2 - 4 * row
    beside = (col + 1 - 2 * parity) * 4 + lane
    docs_dev = lengths.shape[0]
    tokens, model = states.shape
    seq = tokens // docs_dev
    hidden_width = w_gate.shape[1]
    docs = context.shape[0]
    feat = w_out.shape[1] // n
    rows = model // n
    down_rows = hidden_width // n
    pieces = hidden_width // width
    chunks = 2 * pieces
    ny = chunks - nz
    nn = ny - nd

    def peer(d):
        return lax.rem(me + d, n)

    def half_peer(d):
        return lax.rem(half + d, halves)

    def col_peer(d):
        return lax.rem(col + d, cols)

    def remote(src_ref, dst_ref, send_sem, recv_sem, dst):
        return pltpu.make_async_remote_copy(
            src_ref=src_ref, dst_ref=dst_ref, send_sem=send_sem, recv_sem=recv_sem,
            device_id={"dp": dst}, device_id_type=MESH,
        )

    def load(i, src, dst):
        copy = pltpu.make_async_copy(src, dst, in_sem.at[i])
        copy.start()
        return copy

    def load_wide(c):
        at = pl.ds(pl.multiple_of(c * width, width), width)
        return (
            pltpu.make_async_copy(w_gate_in.at[:, at], w_gate.at[:, at], wide_sem.at[0, c]),
            pltpu.make_async_copy(w_up_in.at[:, at], w_up.at[:, at], wide_sem.at[1, c]),
        )

    others = pl.ds(0, n - 1)

    def t_copy(dst, src):
        return remote(t_send.at[dst], t_recv.at[src], all_ssem.at[0], all_rsem.at[0], dst)

    def p_copy(dst, src):
        return remote(p_all.at[src], p_all.at[src], all_ssem.at[1], all_rsem.at[1], dst)

    def g_copy(dst, src):
        return remote(g_all.at[src], g_all.at[src], all_ssem.at[2], all_rsem.at[2], dst)

    def h_copy(dst, src):
        return remote(h_send.at[dst], h_recv.at[src], all_ssem.at[3], all_rsem.at[3], dst)

    t_bytes = remote(t_send.at[others], t_recv.at[others], all_ssem.at[0], all_rsem.at[0], sibling)
    p_bytes = remote(p_all.at[others], p_all.at[others], all_ssem.at[1], all_rsem.at[1], sibling)
    g_bytes = remote(g_all.at[others], g_all.at[others], all_ssem.at[2], all_rsem.at[2], sibling)
    h_bytes = remote(h_send.at[others], h_recv.at[others], all_ssem.at[3], all_rsem.at[3], sibling)

    context_load = load(0, context_in, context)
    w_out_load = load(1, w_out_in, w_out)
    resid_load = load(2, resid_in, resid)
    states_load = load(3, states_in, states)
    for c in range(pieces):
        for copy in load_wide(c):
            copy.start()
    w_down_load = load(4, w_down_in, w_down)

    barrier = pltpu.get_barrier_semaphore()

    @pl.loop(1, n)
    def _(d):
        pl.semaphore_signal(barrier, inc=1, device_id={"dp": peer(d)}, device_id_type=MESH)

    context_load.wait()
    w_out_load.wait()
    resid_load.wait()
    partial = jnp.dot(context[...], w_out[...], preferred_element_type=F32)
    first = (me == 0).astype(F32)
    partial = gain[...].astype(F32).reshape(1, -1) * (partial + first * resid[...].astype(F32))
    for j in range(n):
        t_send[j] = partial[:, j * feat : (j + 1) * feat].astype(BF16)
    t_recv[me] = t_send[me]
    pl.semaphore_wait(barrier, n - 1)

    @pl.loop(1, n)
    def _(d):
        t_copy(peer(d), me).start()

    states_load.wait()
    normed_parts = []
    masks = []
    for d in range(docs_dev):
        x = states[d * seq : (d + 1) * seq].astype(F32)
        inv_rms = lax.rsqrt(jnp.mean(x * x, axis=1, keepdims=True) + EPS)
        normed_wide = x * inv_rms * norm_gain[...].astype(F32).reshape(1, -1)
        normed = normed_wide.astype(BF16)
        normed_parts.append(normed)
        turned = normed.astype(F32).T.astype(BF16)
        for j in range(n):
            feats[j % 2, j // 2 % 2, j // 4 % 2, j // 8, :, d * seq : (d + 1) * seq] = turned[
                j * rows : (j + 1) * rows
            ]
        length = lengths[d]
        mask = (lax.broadcasted_iota(jnp.int32, (seq, 1), 0) < length).astype(F32)
        masks.append(mask)
        s_own[d : d + 1] = jnp.sum(x * mask, axis=0, keepdims=True)
        p_all[me, d : d + 1, model:] = jnp.zeros((1, 128), F32) + length.astype(F32)
    normed = jnp.concatenate(normed_parts, axis=0)
    mask = jnp.concatenate(masks, axis=0)

    feats_copy = remote(feats.at[1 - core], feats_in, feats_sem.at[0], feats_sem.at[1], sibling)
    feats_copy.start()

    def acts_copy(c):
        return remote(acts.at[0, c], acts.at[1, c], ssem.at[0], acts_rsem.at[c], sibling)

    @pl.loop(0, pieces)
    def _(c):
        at = pl.ds(pl.multiple_of(c * width, width), width)
        for copy in load_wide(c):
            copy.wait()
        gate_pre = jnp.dot(normed, w_gate[:, at], preferred_element_type=F32)
        up_pre = jnp.dot(normed, w_up[:, at], preferred_element_type=F32)
        sig = jax.nn.sigmoid(gate_pre)
        silu = gate_pre * sig
        hidden = (silu * up_pre).astype(BF16).astype(F32) * mask
        for d in range(docs_dev):
            h_own[d : d + 1, at] = jnp.sum(
                hidden[d * seq : (d + 1) * seq], axis=0, keepdims=True
            )
        acts[0, c] = (mask * up_pre * sig * (1.0 + gate_pre * (1.0 - sig))).astype(BF16)
        acts[0, c + pieces] = (mask * silu).astype(BF16)

    w_down_load.wait()
    own_parts = jnp.concatenate([part.astype(F32) for part in split3(h_own[...])], axis=0)
    lifted = jnp.dot(own_parts.astype(BF16), w_down[...], preferred_element_type=F32)
    lifted = lifted[:docs_dev] + (lifted[docs_dev : 2 * docs_dev] + lifted[2 * docs_dev :])
    p_all[me, :, :model] = (s_own[...] + lifted) / p_all[me, :, model : model + 1]

    @pl.loop(1, n)
    def _(d):
        p_copy(peer(d), me).start()

    t_bytes.wait_recv()
    scaled = jnp.sum(t_recv[...].astype(F32), axis=0)
    gram_part = lax.dot_general(
        scaled, scaled, (((1,), (1,)), ((), ())), precision=lax.Precision.HIGHEST,
        preferred_element_type=F32,
    )
    fold = max(1, 128 // docs)
    fold_rows = docs // fold
    g_all[me] = jnp.concatenate(
        [gram_part[i * fold_rows : (i + 1) * fold_rows] for i in range(fold)], axis=1
    )

    @pl.loop(1, n)
    def _(d):
        g_copy(peer(d), me).start()

    @pl.loop(0, chunks)
    def _(c):
        acts_copy(c).start()

    h_send[...] = jnp.zeros(h_send.shape, F32)
    for j in range(n):
        h_send[j, :, :down_rows] = h_own[:, j * down_rows : (j + 1) * down_rows]
    h_recv[me] = h_send[me]

    @pl.loop(1, n)
    def _(d):
        h_copy(peer(d), me).start()

    p_bytes.wait_recv()
    for j in range(n):
        big[j * docs_dev : (j + 1) * docs_dev, :] = p_all[j]
    count_all = big[:, model : model + 1]
    pooled = big[:, :model]
    inv_norm = lax.rsqrt(jnp.sum(pooled * pooled, axis=1, keepdims=True) + EPS)
    unit_rows = pooled * inv_norm
    embed = unit_rows.astype(BF16)
    gram_student = rows_product(embed, embed)

    g_bytes.wait_recv()
    folded = jnp.sum(g_all[...], axis=0)
    gram_raw = jnp.concatenate(
        [folded[:, i * docs : (i + 1) * docs] for i in range(fold)], axis=0
    )
    diagonal = lax.broadcasted_iota(jnp.int32, (docs, docs), 0) == lax.broadcasted_iota(
        jnp.int32, (docs, docs), 1
    )
    squares = jnp.where(diagonal, gram_raw, 0.0)
    inv_col = lax.rsqrt(jnp.sum(squares, axis=1, keepdims=True) + EPS)
    inv_row = lax.rsqrt(jnp.sum(squares, axis=0, keepdims=True) + EPS)
    gram_teacher = gram_raw * inv_col * inv_row
    gram_diff = gram_student - gram_teacher

    def total(square):
        return jnp.sum(jnp.sum(square, axis=1, keepdims=True), axis=0, keepdims=True)

    diff_norm = jnp.sqrt(total(gram_diff * gram_diff) + EPS)
    teacher_norm = jnp.sqrt(total(gram_teacher * gram_teacher))
    loss_out[...] = diff_norm / teacher_norm
    d_gram = LOSS_SCALE * gram_diff / (diff_norm * teacher_norm)
    spread = jnp.dot(
        jnp.concatenate(split3(d_gram), axis=0), embed, preferred_element_type=F32
    )
    d_embed = 2.0 * (spread[:docs] + (spread[docs : 2 * docs] + spread[2 * docs :]))
    along = jnp.sum(unit_rows * d_embed, axis=1, keepdims=True)
    d_all = ((d_embed - unit_rows * along) * inv_norm / count_all).astype(BF16)

    pick = lax.broadcasted_iota(jnp.int32, (16, docs), 0)
    wanted = jnp.where(
        pick < docs_dev, me * docs_dev + pick, sibling * docs_dev + pick - docs_dev
    )
    chosen = (wanted == lax.broadcasted_iota(jnp.int32, (16, docs), 1)).astype(F32).astype(BF16)
    d_pair = jnp.dot(chosen, d_all, preferred_element_type=F32).astype(BF16)
    d_pair_hidden = rows_product(d_pair, w_down[...])
    for c in range(chunks):
        at = (c % pieces) * width
        d_hid[c] = d_pair_hidden[:, at : at + width]

    feats_copy.wait_recv()

    def y_copy(c):
        return remote(y_send.at[c], y_recv.at[c], ssem.at[1], y_rsem.at[c], across)

    def n_copy(c):
        return remote(n_send.at[c], n_recv.at[c], ssem.at[2], n_rsem.at[c], beside)

    def z_copy(c, there, src):
        return remote(
            z_send.at[c, there], z_recv.at[c, src], ssem.at[3], z_rsem.at[c],
            (there * 2 + parity) * 4 + lane,
        )

    def d_copy(c, there, src):
        return remote(
            d_send.at[c, there], d_recv.at[c, src], ssem.at[4], d_rsem.at[c], there * 4 + lane
        )

    def zn_copy(c):
        return remote(zn_send.at[c], zn_recv.at[c], ssem.at[5], zn_rsem.at[c], beside)

    def zz_copy(c, there, src):
        return remote(
            zz_send.at[c, :, there], zz_recv.at[c, src], ssem.at[6], zz_rsem.at[c],
            (there * 2 + parity) * 4 + lane,
        )

    def zy_copy(c):
        return remote(zy_send.at[c], zy_recv.at[c], ssem.at[7], zy_rsem.at[c], across)

    def d_acts(c):
        acts_copy(c).wait_recv()
        scaled_acts = []
        for side in range(2):
            for d in range(docs_dev):
                scale = d_hid[c, side * docs_dev + d : side * docs_dev + d + 1]
                part = acts[side, c, d * seq : (d + 1) * seq].astype(F32) * scale
                scaled_acts.append(part.astype(BF16))
        return jnp.concatenate(scaled_acts, axis=0)

    def product(own, given, right):
        left = jnp.concatenate([own.reshape(-1, tokens), given.reshape(-1, tokens)], axis=1)
        both = jnp.dot(left, right, preferred_element_type=F32)
        return both.reshape(2, halves, rows, width)

    def put(c, value):
        at = pl.ds(pl.multiple_of(lax.rem(c, pieces) * width, width), width)
        wide_out[lax.div(c, pieces), :, at] = value

    @pl.loop(0, nz)
    def _(c):
        right = d_acts(c)
        zn_send[c] = product(
            feats[core, :, 1 - parity], feats_in[:, 1 - parity], right
        ).astype(BF16)
        zn_copy(c).start()
        zn_part[c] = product(feats[core, :, parity], feats_in[:, parity], right)

    def zn_done(c):
        zn_copy(c).wait_recv()
        whole = zn_part[c] + zn_recv[c].astype(F32)
        zz_send[c] = whole.astype(BF16)
        zz_part[c] = zn_part[c, :, half] + zn_recv[c, :, half].astype(F32)

        @pl.loop(1, halves)
        def _(d):
            zz_copy(c, half_peer(d), half).start()

    def zz_done(c):
        window = pl.ds(0, halves - 1)
        remote(
            zz_recv.at[c, window], zz_recv.at[c, window], ssem.at[6], zz_rsem.at[c], beside
        ).wait_recv()

        @pl.loop(1, halves)
        def _(d):
            zz_part[c] += zz_recv[c, half_peer(d)].astype(F32)

        zy_send[c] = zz_part[c, 1 - row].astype(BF16)
        zy_copy(c).start()

    def y_start(c):
        right = d_acts(c + nz)
        y_send[c] = product(feats[core, 1 - row], feats_in[1 - row], right).astype(BF16)
        y_copy(c).start()
        y_part[c] = product(feats[core, row], feats_in[row], right)

    def y_done(c):
        y_copy(c).wait_recv()
        y_part[c] += y_recv[c].astype(F32)

    def n_start(c):
        y_done(c)
        n_send[c] = y_part[c, 1 - parity].astype(BF16)
        n_copy(c).start()

    def d_start(c):
        y_done(c + nn)
        for j in range(cols):
            d_send[c, j] = y_part[c + nn, j % 2, j // 2].astype(BF16)

        @pl.loop(1, cols)
        def _(d):
            d_copy(c, col_peer(d), col).start()

    def n_done(c):
        n_copy(c).wait_recv()
        z_send[c] = (y_part[c, parity] + n_recv[c].astype(F32)).astype(BF16)
        z_part[c] = y_part[c, parity, half] + n_recv[c, half].astype(F32)

        @pl.loop(1, halves)
        def _(d):
            z_copy(c, half_peer(d), half).start()

    lag = 3

    @pl.loop(0, lag)
    def _(c):
        y_start(c)

    @pl.loop(lag, ny)
    def _(c):
        y_start(c)
        step = c - lag

        @pl.when(step < nz)
        def _():
            zn_done(step)

        n_start(step)

        @pl.when(step > 0)
        def _():
            n_done(step - 1)

    @pl.loop(0, nz)
    def _(c):
        zz_done(c)

    @pl.loop(ny - lag, nn)
    def _(c):
        n_start(c)
        n_done(c - 1)

    @pl.loop(0, nd)
    def _(c):
        d_start(c)

        @pl.when(c == 0)
        def _():
            n_done(nn - 1)

    h_bytes.wait_recv()
    for j in range(n):
        big_h[j * docs_dev : (j + 1) * docs_dev, :] = h_recv[j]
    sums = jnp.concatenate(split3(big_h[...]), axis=0)
    select = (
        lax.broadcasted_iota(jnp.int32, (down_rows, 128), 0)
        == lax.broadcasted_iota(jnp.int32, (down_rows, 128), 1)
    ).astype(F32).astype(BF16)
    own_sums = rows_product(select, sums).astype(BF16)
    down_out[...] = jnp.dot(
        own_sums, jnp.concatenate([d_all] * 3, axis=0), preferred_element_type=F32
    )

    @pl.loop(0, nn)
    def _(c):
        window = pl.ds(0, halves - 1)
        remote(
            z_recv.at[c, window], z_recv.at[c, window], ssem.at[3], z_rsem.at[c], beside
        ).wait_recv()

        @pl.loop(1, halves)
        def _(d):
            z_part[c] += z_recv[c, half_peer(d)].astype(F32)

        put(c + nz, z_part[c])

    @pl.loop(0, nz)
    def _(c):
        zy_copy(c).wait_recv()
        put(c, zz_part[c, row] + zy_recv[c].astype(F32))

    @pl.loop(0, nd)
    def _(c):
        window = pl.ds(0, cols - 1)
        remote(
            d_recv.at[c, window], d_recv.at[c, window], ssem.at[4], d_rsem.at[c], beside
        ).wait_recv()
        z_part[nn] = y_part[c + nn, parity, half]

        @pl.loop(1, cols)
        def _(d):
            z_part[nn] += d_recv[c, col_peer(d)].astype(F32)

        put(c + nz + nn, z_part[nn])

    feats_copy.wait_send()
    t_bytes.wait_send()
    p_bytes.wait_send()
    g_bytes.wait_send()
    h_bytes.wait_send()
    some = pl.ds(0, halves - 1)
    far = pl.ds(0, cols - 1)
    for i, sent in enumerate((
        acts.at[0], y_send, n_send, z_send.at[:, some], d_send.at[:, far], zn_send,
        zz_send.at[:, :, some], zy_send,
    )):
        remote(sent, sent, ssem.at[i], acts_rsem.at[0], beside).wait_send()


def hand_over(wide, down, gate_out, up_out, down_out, sem):
    copies = [
        pltpu.make_async_copy(made, out, sem.at[i])
        for i, (made, out) in enumerate(
            ((wide.at[0], gate_out), (wide.at[1], up_out), (down, down_out))
        )
    ]
    for copy in copies:
        copy.start()
    for copy in copies:
        copy.wait()


def solution(mesh):
    n = mesh.shape["dp"]
    in_specs = (
        P(("groups", "dp"), None),
        P(("groups", "dp")),
        P(),
        P(),
        P(),
        P(),
        P("groups", "dp"),
        P("dp", None),
        P("groups", None),
        P(),
    )
    out_specs = (
        P("groups"),
        P(("groups", "dp"), None),
        P(("groups", "dp"), None),
        P(("groups", "dp"), None),
    )

    def per_device(
        states, lengths, norm_gain, w_gate, w_up, w_down, context, w_out, resid_stream, teacher_gain
    ):
        tokens, model = states.shape
        hidden_width = w_gate.shape[1]
        docs_dev = lengths.shape[0]
        docs = context.shape[0]
        teacher_width = w_out.shape[1]
        feat = teacher_width // n
        rows = model // n
        width = 256
        chunks = 2 * hidden_width // width
        cols = n // 4
        halves = cols // 2
        nz = 2
        nd = 3
        ny = chunks - nz
        nn = ny - nd
        fold = max(1, 128 // docs)
        packed = model + 128
        hbm = pl.BlockSpec(memory_space=pl.ANY)
        vmem = pl.BlockSpec(memory_space=pltpu.VMEM)
        sem = pltpu.SemaphoreType.DMA
        loss, *made = pl.pallas_call(
            functools.partial(step_kernel, n, width, nz, nd),
            out_shape=(
                jax.ShapeDtypeStruct((1, 1), F32),
                pltpu.VMEM((2, rows, hidden_width), F32),
                pltpu.VMEM((hidden_width // n, model), F32),
            ),
            in_specs=[hbm, pl.BlockSpec(memory_space=pltpu.SMEM), vmem] + [hbm] * 6 + [vmem],
            out_specs=(vmem,) * 3,
            scratch_shapes=[
                pltpu.VMEM((tokens, model), BF16),
                pltpu.VMEM((model, hidden_width), BF16),
                pltpu.VMEM((model, hidden_width), BF16),
                pltpu.VMEM((hidden_width, model), BF16),
                pltpu.VMEM(context.shape, BF16),
                pltpu.VMEM(w_out.shape, BF16),
                pltpu.VMEM(resid_stream.shape, BF16),
                pltpu.VMEM((n, docs, feat), BF16),
                pltpu.VMEM((n, docs, feat), BF16),
                pltpu.VMEM((n, docs // fold, docs * fold), F32),
                pltpu.VMEM((n, docs_dev, packed), F32),
                pltpu.VMEM((docs_dev, hidden_width), F32),
                pltpu.VMEM((n, docs_dev, 128), F32),
                pltpu.VMEM((n, docs_dev, 128), F32),
                pltpu.VMEM((docs_dev, model), F32),
                pltpu.VMEM((docs, packed), F32),
                pltpu.VMEM((docs, 128), F32),
                pltpu.VMEM((2, 2, 2, halves, rows, tokens), BF16),
                pltpu.VMEM((2, 2, halves, rows, tokens), BF16),
                pltpu.VMEM((2, chunks, tokens, width), BF16),
                pltpu.VMEM((chunks, 16, width), F32),
                pltpu.VMEM((ny, 2, halves, rows, width), BF16),
                pltpu.VMEM((ny, 2, halves, rows, width), F32),
                pltpu.VMEM((ny, 2, halves, rows, width), BF16),
                pltpu.VMEM((nn, halves, rows, width), BF16),
                pltpu.VMEM((nn, halves, rows, width), BF16),
                pltpu.VMEM((nn, halves, rows, width), BF16),
                pltpu.VMEM((nn, halves, rows, width), BF16),
                pltpu.VMEM((nn + 1, rows, width), F32),
                pltpu.VMEM((nd, cols, rows, width), BF16),
                pltpu.VMEM((nd, cols, rows, width), BF16),
                pltpu.VMEM((nz, 2, halves, rows, width), BF16),
                pltpu.VMEM((nz, 2, halves, rows, width), BF16),
                pltpu.VMEM((nz, 2, halves, rows, width), F32),
                pltpu.VMEM((nz, 2, halves, rows, width), BF16),
                pltpu.VMEM((nz, halves, 2, rows, width), BF16),
                pltpu.VMEM((nz, 2, rows, width), F32),
                pltpu.VMEM((nz, rows, width), BF16),
                pltpu.VMEM((nz, rows, width), BF16),
                sem((5,)), sem((2, chunks // 2)), sem((4,)), sem((4,)), sem((2,)), sem((8,)),
                sem((chunks,)), sem((ny,)), sem((nn,)), sem((nn,)), sem((nd,)),
                sem((nz,)), sem((nz,)), sem((nz,)),
            ],
            compiler_params=pltpu.CompilerParams(
                collective_id=0, has_side_effects=True, vmem_limit_bytes=56 * 1024 * 1024
            ),
        )(
            states, lengths, norm_gain, w_gate, w_up, w_down, context, w_out,
            resid_stream, teacher_gain,
        )
        made = [pltpu.with_memory_space_constraint(m, pltpu.VMEM) for m in made]
        made = pl.pallas_call(
            hand_over,
            out_shape=(
                jax.ShapeDtypeStruct((rows, hidden_width), F32),
                jax.ShapeDtypeStruct((rows, hidden_width), F32),
                jax.ShapeDtypeStruct((hidden_width // n, model), F32),
            ),
            in_specs=[vmem] * 2,
            out_specs=(hbm,) * 3,
            scratch_shapes=[sem((3,))],
        )(*made)
        return (loss.reshape(1), *made)

    return jax.shard_map(
        per_device, mesh=mesh, in_specs=in_specs, out_specs=out_specs, check_vma=False
    )
```

```python
import functools

import jax
import jax.numpy as jnp
from jax import lax
from jax.experimental import pallas as pl
from jax.experimental.pallas import tpu as pltpu
from jax.sharding import PartitionSpec as P

EPS = 1e-06
LOSS_SCALE = 4096.0
MESH = pl.DeviceIdType.MESH
F32 = jnp.float32
BF16 = jnp.bfloat16


def rows_product(left_rows, right_rows):
    return lax.dot_general(
        left_rows, right_rows, (((1,), (1,)), ((), ())), preferred_element_type=F32
    )


def split3(wide):
    high = wide.astype(BF16)
    rest = wide - high.astype(F32)
    middle = rest.astype(BF16)
    low = (rest - middle.astype(F32)).astype(BF16)
    return high, middle, low


def step_kernel(
    n, width, nz, nd,
    states_in, lengths, norm_gain, w_gate_in, w_up_in, w_down_in, context_in, w_out_in, resid_in, gain,
    loss_out, wide_out, down_out,
    states, w_gate, w_up, w_down, context, w_out, resid,
    t_part, t_in, t_send, t_recv, g_all, p_pair, e_all, lo_all, tall, h_own, h_send, h_recv, s_own, pair, big_h,
    pre, feats, feats_in, acts, d_hid,
    y_send, y_part, y_recv, n_send, n_recv, z_send, z_recv, z_part, d_send, d_recv,
    zn_send, zn_recv, zn_part, zz_send, zz_recv, zz_part, zy_send, zy_recv,
    in_sem, wide_sem, all_ssem, all_rsem, feats_sem, t_sem, p_sem, given_ssem, given_rsem, ssem, acts_rsem,
    y_rsem, n_rsem, z_rsem, d_rsem, zn_rsem, zz_rsem, zy_rsem,
):
    me = lax.axis_index("dp")
    core = lax.rem(me, 2)
    row = lax.rem(lax.div(me, 2), 2)
    col = lax.div(me, 4)
    parity = lax.rem(col, 2)
    half = lax.div(col, 2)
    cols = n // 4
    halves = cols // 2
    lane = row * 2 + core
    sibling = me + 1 - 2 * core
    across = me + 2 - 4 * row
    beside = (col + 1 - 2 * parity) * 4 + lane
    docs_dev = lengths.shape[0]
    tokens, model = states.shape
    seq = tokens // docs_dev
    hidden_width = w_gate.shape[1]
    docs = context.shape[0]
    feat = w_out.shape[1] // n
    rows = model // n
    down_rows = hidden_width // n
    pieces = hidden_width // width
    chunks = 2 * pieces
    ny = chunks - nz
    nn = ny - nd
    lag, n_lag = 3, 1

    def peer(d):
        return lax.rem(me + d, n)

    def half_peer(d):
        return lax.rem(half + d, halves)

    def col_peer(d):
        return lax.rem(col + d, cols)

    def remote(src_ref, dst_ref, send_sem, recv_sem, dst):
        return pltpu.make_async_remote_copy(
            src_ref=src_ref, dst_ref=dst_ref, send_sem=send_sem, recv_sem=recv_sem,
            device_id={"dp": dst}, device_id_type=MESH,
        )

    def load(i, src, dst):
        copy = pltpu.make_async_copy(src, dst, in_sem.at[i])
        copy.start()
        return copy

    def load_wide(c):
        at = pl.ds(pl.multiple_of(c * width, width), width)
        return (
            pltpu.make_async_copy(w_gate_in.at[:, at], w_gate.at[:, at], wide_sem.at[0, c]),
            pltpu.make_async_copy(w_up_in.at[:, at], w_up.at[:, at], wide_sem.at[1, c]),
        )

    others = pl.ds(0, n - 1)
    chip = lax.div(me, 2)
    chips = n // 2
    other_chips = pl.ds(0, chips - 1)

    def chip_peer(d):
        return lax.rem(chip + d, chips)

    def t_copy(dst, src):
        return remote(
            t_send.at[dst], t_recv.at[src], all_ssem.at[0], all_rsem.at[0], 2 * dst + core
        )

    def e_copy(dst, src):
        return remote(e_all.at[src], e_all.at[src], all_ssem.at[1], all_rsem.at[1], dst)

    def g_copy(dst, src):
        return remote(g_all.at[src], g_all.at[src], all_ssem.at[2], all_rsem.at[2], dst)

    def h_copy(dst, src):
        return remote(
            h_send.at[dst], h_recv.at[src, core], all_ssem.at[3], all_rsem.at[3], 2 * dst + core
        )

    def lo_copy(dst, src):
        return remote(
            lo_all.at[src, core], lo_all.at[src, core], all_ssem.at[4], all_rsem.at[4],
            2 * dst + core,
        )

    t_bytes = remote(
        t_send.at[other_chips], t_recv.at[other_chips], all_ssem.at[0], all_rsem.at[0], sibling
    )
    e_bytes = remote(e_all.at[others], e_all.at[others], all_ssem.at[1], all_rsem.at[1], sibling)
    g_bytes = remote(g_all.at[others], g_all.at[others], all_ssem.at[2], all_rsem.at[2], sibling)
    h_bytes = remote(
        h_send.at[other_chips], h_send.at[other_chips], all_ssem.at[3], all_rsem.at[3], sibling
    )
    lo_bytes = remote(
        lo_all.at[other_chips, 0], lo_all.at[other_chips, 0], all_ssem.at[4], all_rsem.at[4],
        sibling,
    )
    h_given = remote(
        h_recv.at[:, core, 1 - core], h_recv.at[:, core, 1 - core], given_ssem.at[0],
        given_rsem.at[0], sibling,
    )
    lo_given = remote(
        lo_all.at[:, core], lo_all.at[:, core], given_ssem.at[1], given_rsem.at[1], sibling
    )
    t_sum = remote(t_part.at[1 - core], t_in, t_sem.at[0], t_sem.at[1], sibling)
    p_copy = remote(p_pair.at[0], p_pair.at[1], p_sem.at[0], p_sem.at[1], sibling)
    spans = model // 128

    def pack(row_values):
        for k in range(spans):
            tall[pl.ds(k, docs_dev, stride=spans), :] = row_values[:, k * 128 : (k + 1) * 128]
        return tall[: docs_dev * spans].astype(BF16)

    def unpack(packed_rows):
        tall[...] = packed_rows.reshape(docs * spans, 128).astype(F32)
        return jnp.concatenate(
            [tall[pl.ds(k, docs, stride=spans), :] for k in range(spans)], axis=1
        ).astype(BF16)

    context_load = load(0, context_in, context)
    w_out_load = load(1, w_out_in, w_out)
    resid_load = load(2, resid_in, resid)
    states_load = load(3, states_in, states)
    for c in range(pieces):
        for copy in load_wide(c):
            copy.start()
    w_down_load = load(4, w_down_in, w_down)

    barrier = pltpu.get_barrier_semaphore()

    @pl.loop(1, n)
    def _(d):
        pl.semaphore_signal(barrier, inc=1, device_id={"dp": peer(d)}, device_id_type=MESH)

    context_load.wait()
    w_out_load.wait()
    resid_load.wait()
    partial = jnp.dot(context[...], w_out[...], preferred_element_type=F32)
    first = (me == 0).astype(F32)
    partial = gain[...].astype(F32).reshape(1, -1) * (partial + first * resid[...].astype(F32))
    for j in range(n):
        t_part[j % 2, j // 2] = partial[:, j * feat : (j + 1) * feat]
    pl.semaphore_wait(barrier, n - 1)
    t_sum.start()

    states_load.wait()
    normed_parts = []
    masks = []
    for d in range(docs_dev):
        x = states[d * seq : (d + 1) * seq].astype(F32)
        inv_rms = lax.rsqrt(jnp.mean(x * x, axis=1, keepdims=True) + EPS)
        normed_wide = x * inv_rms * norm_gain[...].astype(F32).reshape(1, -1)
        normed = normed_wide.astype(BF16)
        normed_parts.append(normed)
        length = lengths[d]
        mask = (lax.broadcasted_iota(jnp.int32, (seq, 1), 0) < length).astype(F32)
        masks.append(mask)
        s_own[d : d + 1] = jnp.sum(x * mask, axis=0, keepdims=True)
        p_pair[0, d : d + 1, model:] = jnp.zeros((1, 128), F32) + length.astype(F32)
    normed = jnp.concatenate(normed_parts, axis=0)
    mask = jnp.concatenate(masks, axis=0)

    feats_copy = remote(feats.at[1 - core], feats_in, feats_sem.at[0], feats_sem.at[1], sibling)

    def acts_copy(c):
        return remote(acts.at[0, c], acts.at[1, c], ssem.at[0], acts_rsem.at[c], sibling)

    def forward(c):
        at = slice(c * width, (c + 1) * width)
        gate_pre = jnp.dot(normed, w_gate[:, at], preferred_element_type=F32)
        up_pre = jnp.dot(normed, w_up[:, at], preferred_element_type=F32)
        pre[0, c] = gate_pre
        pre[1, c] = up_pre
        hidden = (gate_pre * jax.nn.sigmoid(gate_pre) * up_pre).astype(BF16).astype(F32) * mask
        for d in range(docs_dev):
            h_own[d : d + 1, at] = jnp.sum(
                hidden[d * seq : (d + 1) * seq], axis=0, keepdims=True
            )

    def wide_wait(c):
        for copy in load_wide(c):
            copy.wait()

    wide_wait(0)
    forward(0)
    t_sum.wait_recv()
    t_send[...] = (t_part[core] + t_in[...]).astype(BF16)
    t_recv[chip] = t_send[chip]

    @pl.loop(1, chips)
    def _(d):
        t_copy(chip_peer(d), chip).start()

    for c in range(1, pieces):
        wide_wait(c)
    for c in range(1, pieces):
        forward(c)

    w_down_load.wait()
    own_parts = jnp.concatenate([part.astype(F32) for part in split3(h_own[...])], axis=0)
    lifted = jnp.dot(own_parts.astype(BF16), w_down[...], preferred_element_type=F32)
    lifted = lifted[:docs_dev] + (lifted[docs_dev : 2 * docs_dev] + lifted[2 * docs_dev :])
    own_pooled = (s_own[...] + lifted) / p_pair[0, :, model : model + 1]
    p_pair[0, :, :model] = own_pooled
    p_copy.start()
    own_inv = lax.rsqrt(jnp.sum(own_pooled * own_pooled, axis=1, keepdims=True) + EPS)
    own_unit = own_pooled * own_inv
    e_all[me] = pack(own_unit)

    @pl.loop(1, n)
    def _(d):
        e_copy(peer(d), me).start()

    t_bytes.wait_recv()
    scaled = jnp.sum(t_recv[...].astype(F32), axis=0)
    gram_part = lax.dot_general(
        scaled, scaled, (((1,), (1,)), ((), ())), precision=lax.Precision.HIGHEST,
        preferred_element_type=F32,
    )
    fold = max(1, 128 // docs)
    fold_rows = docs // fold
    g_all[me] = jnp.concatenate(
        [gram_part[i * fold_rows : (i + 1) * fold_rows] for i in range(fold)], axis=1
    )

    @pl.loop(1, n)
    def _(d):
        g_copy(peer(d), me).start()

    for d in range(docs_dev):
        turned = normed_parts[d].astype(F32).T.astype(BF16)
        for j in range(n):
            feats[j % 2, j // 2 % 2, j // 4 % 2, j // 8, :, d * seq : (d + 1) * seq] = turned[
                j * rows : (j + 1) * rows
            ]
    feats_copy.start()

    def acts_start(c):
        gate_pre = pre[0, c]
        sig = jax.nn.sigmoid(gate_pre)
        acts[0, 2 * c] = (mask * pre[1, c] * sig * (1.0 + gate_pre * (1.0 - sig))).astype(BF16)
        acts[0, 2 * c + 1] = (mask * (gate_pre * sig)).astype(BF16)
        acts_copy(2 * c).start()
        acts_copy(2 * c + 1).start()

    first = nz
    early = (nz + first + 1) // 2

    @pl.loop(0, early)
    def _(c):
        acts_start(c)

    scale = own_inv / p_pair[0, :, model : model + 1] + jnp.zeros((docs_dev, 128 - down_rows), F32)
    for j in range(n):
        h_send[j // 2, j % 2, :, :down_rows] = h_own[:, j * down_rows : (j + 1) * down_rows]
        h_send[j // 2, j % 2, :, down_rows:] = scale
    h_recv[chip, core] = h_send[chip]
    lo_all[chip, core] = pack(own_unit - own_unit.astype(BF16).astype(F32))

    @pl.loop(1, chips)
    def _(d):
        h_copy(chip_peer(d), chip).start()
        lo_copy(chip_peer(d), chip).start()

    pair[...] = jnp.ones(pair.shape, F32)
    pair[:docs_dev] = p_pair[0]
    p_copy.wait_recv()
    pair[docs_dev : 2 * docs_dev] = p_pair[1]
    pooled = pair[:, :model]
    inv_norm = lax.rsqrt(jnp.sum(pooled * pooled, axis=1, keepdims=True) + EPS)
    unit_rows = pooled * inv_norm
    inv_count = inv_norm / pair[:, model : model + 1]

    e_bytes.wait_recv()
    embed = unpack(e_all[...])
    gram_student = rows_product(embed, embed)

    g_bytes.wait_recv()
    folded = jnp.sum(g_all[...], axis=0)
    gram_raw = jnp.concatenate(
        [folded[:, i * docs : (i + 1) * docs] for i in range(fold)], axis=0
    )
    diagonal = lax.broadcasted_iota(jnp.int32, (docs, docs), 0) == lax.broadcasted_iota(
        jnp.int32, (docs, docs), 1
    )
    squares = jnp.where(diagonal, gram_raw, 0.0)
    inv_col = lax.rsqrt(jnp.sum(squares, axis=1, keepdims=True) + EPS)
    inv_row = lax.rsqrt(jnp.sum(squares, axis=0, keepdims=True) + EPS)
    gram_teacher = gram_raw * inv_col * inv_row
    gram_diff = gram_student - gram_teacher

    def total(square):
        return jnp.sum(jnp.sum(square, axis=1, keepdims=True), axis=0, keepdims=True)

    diff_norm = jnp.sqrt(total(gram_diff * gram_diff) + EPS)
    teacher_norm = jnp.sqrt(total(gram_teacher * gram_teacher))
    loss_out[...] = diff_norm / teacher_norm
    d_gram = LOSS_SCALE * gram_diff / (diff_norm * teacher_norm)
    doc_at = lax.broadcasted_iota(jnp.int32, (docs, docs), 0)
    chosen = [
        jnp.sum(jnp.where(doc_at == owner * docs_dev + d, d_gram, 0.0), axis=0, keepdims=True)
        for owner in (me, sibling)
        for d in range(docs_dev)
    ]
    chosen.append(jnp.zeros((16 - 2 * docs_dev, docs), F32))
    spread = jnp.dot(
        jnp.concatenate(split3(jnp.concatenate(chosen, axis=0)), axis=0), embed,
        preferred_element_type=F32,
    )
    d_embed = 2.0 * (spread[:16] + (spread[16:32] + spread[32:]))
    along = jnp.sum(unit_rows * d_embed, axis=1, keepdims=True)
    d_wide = (d_embed - unit_rows * along) * inv_count
    d_pair = d_wide.astype(BF16)
    d_pair_hidden = rows_product(d_pair, w_down[...])
    for c in range(chunks):
        at = (c // 2) * width
        d_hid[c] = d_pair_hidden[:, at : at + width]

    feats_copy.wait_recv()

    def y_copy(c):
        return remote(y_send.at[c], y_recv.at[c], ssem.at[1], y_rsem.at[c], across)

    def n_copy(c):
        return remote(n_send.at[c], n_recv.at[c], ssem.at[2], n_rsem.at[c], beside)

    def z_copy(c, there, src):
        return remote(
            z_send.at[c, there], z_recv.at[c, src], ssem.at[3], z_rsem.at[c],
            (there * 2 + parity) * 4 + lane,
        )

    def d_copy(c, there, src):
        return remote(
            d_send.at[c, there], d_recv.at[c, src], ssem.at[4], d_rsem.at[c], there * 4 + lane
        )

    def zn_copy(c):
        return remote(zn_send.at[c], zn_recv.at[c], ssem.at[5], zn_rsem.at[c], beside)

    def zz_copy(c, there, src):
        return remote(
            zz_send.at[c, :, there], zz_recv.at[c, src], ssem.at[6], zz_rsem.at[c],
            (there * 2 + parity) * 4 + lane,
        )

    def zy_copy(c):
        return remote(zy_send.at[c], zy_recv.at[c], ssem.at[7], zy_rsem.at[c], across)

    def d_acts(c):
        acts_copy(c).wait_recv()
        scaled_acts = []
        for side in range(2):
            for d in range(docs_dev):
                scale = d_hid[c, side * docs_dev + d : side * docs_dev + d + 1]
                part = acts[side, c, d * seq : (d + 1) * seq].astype(F32) * scale
                scaled_acts.append(part.astype(BF16))
        return jnp.concatenate(scaled_acts, axis=0)

    def product(own, given, right):
        left = jnp.concatenate([own.reshape(-1, tokens), given.reshape(-1, tokens)], axis=1)
        both = jnp.dot(left, right, preferred_element_type=F32)
        return both.reshape(2, halves, rows, width)

    def put(c, value):
        at = pl.ds(pl.multiple_of(lax.div(c, 2) * width, width), width)
        wide_out[lax.rem(c, 2), :, at] = value

    def z_start(c):
        right = d_acts(c)
        zn_send[c] = product(
            feats[core, :, 1 - parity], feats_in[:, 1 - parity], right
        ).astype(BF16)
        zn_copy(c).start()
        zn_part[c] = product(feats[core, :, parity], feats_in[:, parity], right)

    def zn_done(c):
        zn_copy(c).wait_recv()
        whole = zn_part[c] + zn_recv[c].astype(F32)
        zz_send[c] = whole.astype(BF16)
        zz_part[c] = zn_part[c, :, half] + zn_recv[c, :, half].astype(F32)

        @pl.loop(1, halves)
        def _(d):
            zz_copy(c, half_peer(d), half).start()

    def zz_done(c):
        window = pl.ds(0, halves - 1)
        remote(
            zz_recv.at[c, window], zz_recv.at[c, window], ssem.at[6], zz_rsem.at[c], beside
        ).wait_recv()

        @pl.loop(1, halves)
        def _(d):
            zz_part[c] += zz_recv[c, half_peer(d)].astype(F32)

        zy_send[c] = zz_part[c, 1 - row].astype(BF16)
        zy_copy(c).start()

    def y_start(c):
        right = d_acts(c + nz)
        y_send[c] = product(feats[core, 1 - row], feats_in[1 - row], right).astype(BF16)
        y_copy(c).start()
        y_part[c] = product(feats[core, row], feats_in[row], right)

    def y_done(c):
        y_copy(c).wait_recv()
        y_part[c] += y_recv[c].astype(F32)

    def n_start(c):
        y_done(c)
        n_send[c] = y_part[c, 1 - parity].astype(BF16)
        n_copy(c).start()

    def d_start(c):
        y_done(c + nn)
        for j in range(cols):
            d_send[c, j] = y_part[c + nn, j % 2, j // 2].astype(BF16)

        @pl.loop(1, cols)
        def _(d):
            d_copy(c, col_peer(d), col).start()

    def n_done(c):
        n_copy(c).wait_recv()
        z_send[c] = (y_part[c, parity] + n_recv[c].astype(F32)).astype(BF16)
        z_part[c] = y_part[c, parity, half] + n_recv[c, half].astype(F32)

        @pl.loop(1, halves)
        def _(d):
            z_copy(c, half_peer(d), half).start()

    def within(i, count, run):
        @pl.when(jnp.logical_and(i >= 0, i < count))
        def _():
            run(i)


    def advance(c):
        within(c, ny, y_start)
        within(c, nz, z_start)
        step = c - lag
        within(step, nz, zn_done)
        within(step, nn, n_start)
        within(step - nn, nd, d_start)
        within(step - n_lag, nn, n_done)
        within(c - ny, nz, zz_done)

    @pl.loop(0, first)
    def _(c):
        y_start(c)
        within(c, nz, z_start)

    @pl.loop(early, pieces)
    def _(c):
        acts_start(c)

    @pl.loop(first, lag)
    def _(c):
        y_start(c)

    h_bytes.wait_recv()
    h_given.start()
    lo_bytes.wait_recv()
    lo_given.start()

    @pl.loop(lag, ny + lag)
    def _(c):
        advance(c)

    @pl.loop(ny - n_lag, nn)
    def _(c):
        n_done(c)

    @pl.loop(lag, nz)
    def _(c):
        zz_done(c)

    h_given.wait_recv()
    for j in range(n):
        big_h[j * docs_dev : (j + 1) * docs_dev, :] = h_recv[j // 2, j % 2, core]
    sums = jnp.concatenate(split3(big_h[...]), axis=0)
    select = (
        lax.broadcasted_iota(jnp.int32, (down_rows, 128), 0)
        == lax.broadcasted_iota(jnp.int32, (down_rows, 128), 1)
    ).astype(F32).astype(BF16)
    own_sums = rows_product(select, sums).astype(BF16)
    lo_given.wait_recv()
    units = embed.astype(F32) + unpack(lo_all[...]).astype(F32)
    spread = jnp.dot(
        jnp.concatenate(split3(d_gram), axis=0), embed, preferred_element_type=F32
    )
    d_embed = 2.0 * (spread[:docs] + (spread[docs : 2 * docs] + spread[2 * docs :]))
    along = jnp.sum(units * d_embed, axis=1, keepdims=True)
    d_all = ((d_embed - units * along) * big_h[:, down_rows : down_rows + 1]).astype(BF16)
    down_out[...] = jnp.dot(
        own_sums, jnp.concatenate([d_all] * 3, axis=0), preferred_element_type=F32
    )

    @pl.loop(0, nn)
    def _(c):
        window = pl.ds(0, halves - 1)
        remote(
            z_recv.at[c, window], z_recv.at[c, window], ssem.at[3], z_rsem.at[c], beside
        ).wait_recv()

        @pl.loop(1, halves)
        def _(d):
            z_part[c] += z_recv[c, half_peer(d)].astype(F32)

        put(c + nz, z_part[c])

    @pl.loop(0, nz)
    def _(c):
        zy_copy(c).wait_recv()
        put(c, zz_part[c, row] + zy_recv[c].astype(F32))

    @pl.loop(0, nd)
    def _(c):
        window = pl.ds(0, cols - 1)
        remote(
            d_recv.at[c, window], d_recv.at[c, window], ssem.at[4], d_rsem.at[c], beside
        ).wait_recv()
        z_part[nn] = y_part[c + nn, parity, half]

        @pl.loop(1, cols)
        def _(d):
            z_part[nn] += d_recv[c, col_peer(d)].astype(F32)

        put(c + nz + nn, z_part[nn])

    feats_copy.wait_send()
    t_bytes.wait_send()
    e_bytes.wait_send()
    lo_bytes.wait_send()
    h_given.wait_send()
    lo_given.wait_send()
    t_sum.wait_send()
    p_copy.wait_send()
    g_bytes.wait_send()
    h_bytes.wait_send()
    some = pl.ds(0, halves - 1)
    far = pl.ds(0, cols - 1)
    for i, sent in enumerate((
        acts.at[0], y_send, n_send, z_send.at[:, some], d_send.at[:, far], zn_send,
        zz_send.at[:, :, some], zy_send,
    )):
        remote(sent, sent, ssem.at[i], acts_rsem.at[0], beside).wait_send()


def hand_over(wide, down, gate_out, up_out, down_out, sem):
    copies = [
        pltpu.make_async_copy(made, out, sem.at[i])
        for i, (made, out) in enumerate(
            ((wide.at[0], gate_out), (wide.at[1], up_out), (down, down_out))
        )
    ]
    for copy in copies:
        copy.start()
    for copy in copies:
        copy.wait()


def solution(mesh):
    n = mesh.shape["dp"]
    in_specs = (
        P(("groups", "dp"), None),
        P(("groups", "dp")),
        P(),
        P(),
        P(),
        P(),
        P("groups", "dp"),
        P("dp", None),
        P("groups", None),
        P(),
    )
    out_specs = (
        P("groups"),
        P(("groups", "dp"), None),
        P(("groups", "dp"), None),
        P(("groups", "dp"), None),
    )

    def per_device(
        states, lengths, norm_gain, w_gate, w_up, w_down, context, w_out, resid_stream, teacher_gain
    ):
        tokens, model = states.shape
        hidden_width = w_gate.shape[1]
        docs_dev = lengths.shape[0]
        docs = context.shape[0]
        teacher_width = w_out.shape[1]
        feat = teacher_width // n
        rows = model // n
        width = 256
        chunks = 2 * hidden_width // width
        cols = n // 4
        halves = cols // 2
        nz = 2
        nd = 2
        ny = chunks - nz
        nn = ny - nd
        fold = max(1, 128 // docs)
        packed = model + 128
        hbm = pl.BlockSpec(memory_space=pl.ANY)
        vmem = pl.BlockSpec(memory_space=pltpu.VMEM)
        sem = pltpu.SemaphoreType.DMA
        loss, *made = pl.pallas_call(
            functools.partial(step_kernel, n, width, nz, nd),
            out_shape=(
                jax.ShapeDtypeStruct((1, 1), F32),
                pltpu.VMEM((2, rows, hidden_width), F32),
                pltpu.VMEM((hidden_width // n, model), F32),
            ),
            in_specs=[hbm, pl.BlockSpec(memory_space=pltpu.SMEM), vmem] + [hbm] * 6 + [vmem],
            out_specs=(vmem,) * 3,
            scratch_shapes=[
                pltpu.VMEM((tokens, model), BF16),
                pltpu.VMEM((model, hidden_width), BF16),
                pltpu.VMEM((model, hidden_width), BF16),
                pltpu.VMEM((hidden_width, model), BF16),
                pltpu.VMEM(context.shape, BF16),
                pltpu.VMEM(w_out.shape, BF16),
                pltpu.VMEM(resid_stream.shape, BF16),
                pltpu.VMEM((2, n // 2, docs, feat), F32),
                pltpu.VMEM((n // 2, docs, feat), F32),
                pltpu.VMEM((n // 2, docs, feat), BF16),
                pltpu.VMEM((n // 2, docs, feat), BF16),
                pltpu.VMEM((n, docs // fold, docs * fold), F32),
                pltpu.VMEM((2, docs_dev, packed), F32),
                pltpu.VMEM((n, docs_dev * model // 128, 128), BF16),
                pltpu.VMEM((n // 2, 2, docs_dev * model // 128, 128), BF16),
                pltpu.VMEM((docs * model // 128, 128), F32),
                pltpu.VMEM((docs_dev, hidden_width), F32),
                pltpu.VMEM((n // 2, 2, docs_dev, 128), F32),
                pltpu.VMEM((n // 2, 2, 2, docs_dev, 128), F32),
                pltpu.VMEM((docs_dev, model), F32),
                pltpu.VMEM((16, packed), F32),
                pltpu.VMEM((docs, 128), F32),
                pltpu.VMEM((2, hidden_width // width, tokens, width), F32),
                pltpu.VMEM((2, 2, 2, halves, rows, tokens), BF16),
                pltpu.VMEM((2, 2, halves, rows, tokens), BF16),
                pltpu.VMEM((2, chunks, tokens, width), BF16),
                pltpu.VMEM((chunks, 16, width), F32),
                pltpu.VMEM((ny, 2, halves, rows, width), BF16),
                pltpu.VMEM((ny, 2, halves, rows, width), F32),
                pltpu.VMEM((ny, 2, halves, rows, width), BF16),
                pltpu.VMEM((nn, halves, rows, width), BF16),
                pltpu.VMEM((nn, halves, rows, width), BF16),
                pltpu.VMEM((nn, halves, rows, width), BF16),
                pltpu.VMEM((nn, halves, rows, width), BF16),
                pltpu.VMEM((nn + 1, rows, width), F32),
                pltpu.VMEM((nd, cols, rows, width), BF16),
                pltpu.VMEM((nd, cols, rows, width), BF16),
                pltpu.VMEM((nz, 2, halves, rows, width), BF16),
                pltpu.VMEM((nz, 2, halves, rows, width), BF16),
                pltpu.VMEM((nz, 2, halves, rows, width), F32),
                pltpu.VMEM((nz, 2, halves, rows, width), BF16),
                pltpu.VMEM((nz, halves, 2, rows, width), BF16),
                pltpu.VMEM((nz, 2, rows, width), F32),
                pltpu.VMEM((nz, rows, width), BF16),
                pltpu.VMEM((nz, rows, width), BF16),
                sem((5,)), sem((2, chunks // 2)), sem((5,)), sem((5,)), sem((2,)), sem((2,)), sem((2,)), sem((2,)), sem((2,)), sem((8,)),
                sem((chunks,)), sem((ny,)), sem((nn,)), sem((nn,)), sem((nd,)),
                sem((nz,)), sem((nz,)), sem((nz,)),
            ],
            compiler_params=pltpu.CompilerParams(
                collective_id=0, has_side_effects=True, vmem_limit_bytes=56 * 1024 * 1024
            ),
        )(
            states, lengths, norm_gain, w_gate, w_up, w_down, context, w_out,
            resid_stream, teacher_gain,
        )
        made = [pltpu.with_memory_space_constraint(m, pltpu.VMEM) for m in made]
        made = pl.pallas_call(
            hand_over,
            out_shape=(
                jax.ShapeDtypeStruct((rows, hidden_width), F32),
                jax.ShapeDtypeStruct((rows, hidden_width), F32),
                jax.ShapeDtypeStruct((hidden_width // n, model), F32),
            ),
            in_specs=[vmem] * 2,
            out_specs=(hbm,) * 3,
            scratch_shapes=[sem((3,))],
        )(*made)
        return (loss.reshape(1), *made)

    return jax.shard_map(
        per_device, mesh=mesh, in_specs=in_specs, out_specs=out_specs, check_vma=False
    )
```

```python
import functools

import jax
import jax.numpy as jnp
from jax import lax
from jax.experimental import pallas as pl
from jax.experimental.pallas import tpu as pltpu
from jax.sharding import PartitionSpec as P

EPS = 1e-06
LOSS_SCALE = 4096.0
MESH = pl.DeviceIdType.MESH
F32 = jnp.float32
BF16 = jnp.bfloat16


def rows_product(left_rows, right_rows):
    return lax.dot_general(
        left_rows, right_rows, (((1,), (1,)), ((), ())), preferred_element_type=F32
    )


def split3(wide):
    high = wide.astype(BF16)
    rest = wide - high.astype(F32)
    middle = rest.astype(BF16)
    low = (rest - middle.astype(F32)).astype(BF16)
    return high, middle, low


def step_kernel(
    n, width, nz, nd,
    states_in, lengths, norm_gain, w_gate_in, w_up_in, w_down_in, context_in, w_out_in, resid_in, gain,
    loss_out, wide_out, down_out,
    states, w_gate, w_up, w_down, context, w_out, resid,
    t_part, t_in, t_send, t_recv, g_all, p_pair, e_all, lo_all, tall, h_own, h_send, h_recv, s_own, pair, big_h,
    pre, feats, feats_in, acts, d_hid,
    y_send, y_part, y_recv, n_send, n_recv, z_send, z_recv, z_part, d_send, d_recv, d_part,
    zn_send, zn_recv, zn_part, zz_send, zz_recv, zz_part, zy_send, zy_recv,
    in_sem, wide_sem, all_ssem, all_rsem, feats_sem, t_sem, p_sem, given_ssem, given_rsem, ssem, acts_rsem,
    y_rsem, ys_rsem, n_rsem, z_rsem, d_rsem, zn_rsem, zz_rsem, zy_rsem,
):
    me = lax.axis_index("dp")
    core = lax.rem(me, 2)
    row = lax.rem(lax.div(me, 2), 2)
    col = lax.div(me, 4)
    parity = lax.rem(col, 2)
    half = lax.div(col, 2)
    cols = n // 4
    halves = cols // 2
    lane = row * 2 + core
    sibling = me + 1 - 2 * core
    across = me + 2 - 4 * row
    beside = (col + 1 - 2 * parity) * 4 + lane
    docs_dev = lengths.shape[0]
    tokens, model = states.shape
    seq = tokens // docs_dev
    hidden_width = w_gate.shape[1]
    docs = context.shape[0]
    feat = w_out.shape[1] // n
    rows = model // n
    down_rows = hidden_width // n
    pieces = hidden_width // width
    chunks = 2 * pieces
    ny = chunks - nz
    nn = ny - nd
    lag, n_lag, z_lag = 3, 1, 4

    def peer(d):
        return lax.rem(me + d, n)

    def half_peer(d):
        return lax.rem(half + d, halves)

    def col_peer(d):
        return lax.rem(col + d, cols)

    high = half * 2 // halves

    def far_first(i, count):
        return (1 - high) * (count - 1 - i) + high * (1 + i)

    def remote(src_ref, dst_ref, send_sem, recv_sem, dst):
        return pltpu.make_async_remote_copy(
            src_ref=src_ref, dst_ref=dst_ref, send_sem=send_sem, recv_sem=recv_sem,
            device_id={"dp": dst}, device_id_type=MESH,
        )

    def load(i, src, dst):
        copy = pltpu.make_async_copy(src, dst, in_sem.at[i])
        copy.start()
        return copy

    def load_wide(c):
        at = pl.ds(pl.multiple_of(c * width, width), width)
        return (
            pltpu.make_async_copy(w_gate_in.at[:, at], w_gate.at[:, at], wide_sem.at[0, c]),
            pltpu.make_async_copy(w_up_in.at[:, at], w_up.at[:, at], wide_sem.at[1, c]),
        )

    others = pl.ds(0, n - 1)
    chip = lax.div(me, 2)
    chips = n // 2
    other_chips = pl.ds(0, chips - 1)

    def chip_peer(d):
        return lax.rem(chip + d, chips)

    def t_copy(dst, src):
        return remote(
            t_send.at[dst], t_recv.at[src], all_ssem.at[0], all_rsem.at[0], 2 * dst + core
        )

    def e_copy(dst, src):
        return remote(e_all.at[src], e_all.at[src], all_ssem.at[1], all_rsem.at[1], dst)

    def g_copy(dst, src):
        return remote(g_all.at[src], g_all.at[src], all_ssem.at[2], all_rsem.at[2], dst)

    def h_copy(dst, src):
        return remote(
            h_send.at[dst], h_recv.at[src, core], all_ssem.at[3], all_rsem.at[3], 2 * dst + core
        )

    def lo_copy(dst, src):
        return remote(
            lo_all.at[src, core], lo_all.at[src, core], all_ssem.at[4], all_rsem.at[4],
            2 * dst + core,
        )

    t_bytes = remote(
        t_send.at[other_chips], t_recv.at[other_chips], all_ssem.at[0], all_rsem.at[0], sibling
    )
    e_bytes = remote(e_all.at[others], e_all.at[others], all_ssem.at[1], all_rsem.at[1], sibling)
    g_bytes = remote(g_all.at[others], g_all.at[others], all_ssem.at[2], all_rsem.at[2], sibling)
    h_bytes = remote(
        h_send.at[other_chips], h_send.at[other_chips], all_ssem.at[3], all_rsem.at[3], sibling
    )
    lo_bytes = remote(
        lo_all.at[other_chips, 0], lo_all.at[other_chips, 0], all_ssem.at[4], all_rsem.at[4],
        sibling,
    )
    h_given = remote(
        h_recv.at[:, core, 1 - core], h_recv.at[:, core, 1 - core], given_ssem.at[0],
        given_rsem.at[0], sibling,
    )
    lo_given = remote(
        lo_all.at[:, core], lo_all.at[:, core], given_ssem.at[1], given_rsem.at[1], sibling
    )
    t_sum = remote(t_part.at[1 - core], t_in, t_sem.at[0], t_sem.at[1], sibling)
    p_copy = remote(p_pair.at[0], p_pair.at[1], p_sem.at[0], p_sem.at[1], sibling)
    spans = model // 128

    def pack(row_values):
        for k in range(spans):
            tall[pl.ds(k, docs_dev, stride=spans), :] = row_values[:, k * 128 : (k + 1) * 128]
        return tall[: docs_dev * spans].astype(BF16)

    def unpack(packed_rows):
        tall[...] = packed_rows.reshape(docs * spans, 128).astype(F32)
        return jnp.concatenate(
            [tall[pl.ds(k, docs, stride=spans), :] for k in range(spans)], axis=1
        ).astype(BF16)

    context_load = load(0, context_in, context)
    w_out_load = load(1, w_out_in, w_out)
    resid_load = load(2, resid_in, resid)
    states_load = load(3, states_in, states)
    for c in range(pieces):
        for copy in load_wide(c):
            copy.start()
    w_down_load = load(4, w_down_in, w_down)

    barrier = pltpu.get_barrier_semaphore()

    @pl.loop(1, n)
    def _(d):
        pl.semaphore_signal(barrier, inc=1, device_id={"dp": peer(d)}, device_id_type=MESH)

    context_load.wait()
    w_out_load.wait()
    resid_load.wait()
    partial = jnp.dot(context[...], w_out[...], preferred_element_type=F32)
    first = (me == 0).astype(F32)
    partial = gain[...].astype(F32).reshape(1, -1) * (partial + first * resid[...].astype(F32))
    for j in range(n):
        t_part[j % 2, j // 2] = partial[:, j * feat : (j + 1) * feat]
    pl.semaphore_wait(barrier, n - 1)
    t_sum.start()

    states_load.wait()
    normed_parts = []
    masks = []
    for d in range(docs_dev):
        x = states[d * seq : (d + 1) * seq].astype(F32)
        inv_rms = lax.rsqrt(jnp.mean(x * x, axis=1, keepdims=True) + EPS)
        normed_wide = x * inv_rms * norm_gain[...].astype(F32).reshape(1, -1)
        normed = normed_wide.astype(BF16)
        normed_parts.append(normed)
        length = lengths[d]
        mask = (lax.broadcasted_iota(jnp.int32, (seq, 1), 0) < length).astype(F32)
        masks.append(mask)
        s_own[d : d + 1] = jnp.sum(x * mask, axis=0, keepdims=True)
        p_pair[0, d : d + 1, model:] = jnp.zeros((1, 128), F32) + length.astype(F32)
    normed = jnp.concatenate(normed_parts, axis=0)
    mask = jnp.concatenate(masks, axis=0)

    feats_copy = remote(feats.at[1 - core], feats_in, feats_sem.at[0], feats_sem.at[1], sibling)

    def acts_copy(c):
        return remote(acts.at[0, c], acts.at[1, c], ssem.at[0], acts_rsem.at[c], sibling)

    def forward(c):
        at = slice(c * width, (c + 1) * width)
        gate_pre = jnp.dot(normed, w_gate[:, at], preferred_element_type=F32)
        up_pre = jnp.dot(normed, w_up[:, at], preferred_element_type=F32)
        pre[0, c] = gate_pre
        pre[1, c] = up_pre
        hidden = (gate_pre * jax.nn.sigmoid(gate_pre) * up_pre).astype(BF16).astype(F32) * mask
        for d in range(docs_dev):
            h_own[d : d + 1, at] = jnp.sum(
                hidden[d * seq : (d + 1) * seq], axis=0, keepdims=True
            )

    def wide_wait(c):
        for copy in load_wide(c):
            copy.wait()

    wide_wait(0)
    forward(0)
    t_sum.wait_recv()
    t_send[...] = (t_part[core] + t_in[...]).astype(BF16)
    t_recv[chip] = t_send[chip]

    @pl.loop(1, chips)
    def _(d):
        t_copy(chip_peer(d), chip).start()

    for c in range(1, pieces):
        wide_wait(c)
    for c in range(1, pieces):
        forward(c)

    w_down_load.wait()
    own_parts = jnp.concatenate([part.astype(F32) for part in split3(h_own[...])], axis=0)
    lifted = jnp.dot(own_parts.astype(BF16), w_down[...], preferred_element_type=F32)
    lifted = lifted[:docs_dev] + (lifted[docs_dev : 2 * docs_dev] + lifted[2 * docs_dev :])
    own_pooled = (s_own[...] + lifted) / p_pair[0, :, model : model + 1]
    p_pair[0, :, :model] = own_pooled
    p_copy.start()
    own_inv = lax.rsqrt(jnp.sum(own_pooled * own_pooled, axis=1, keepdims=True) + EPS)
    own_unit = own_pooled * own_inv
    e_all[me] = pack(own_unit)

    @pl.loop(1, n)
    def _(d):
        e_copy(peer(d), me).start()

    t_bytes.wait_recv()
    scaled = jnp.sum(t_recv[...].astype(F32), axis=0)
    gram_part = lax.dot_general(
        scaled, scaled, (((1,), (1,)), ((), ())), precision=lax.Precision.HIGHEST,
        preferred_element_type=F32,
    )
    fold = max(1, 128 // docs)
    fold_rows = docs // fold
    g_all[me] = jnp.concatenate(
        [gram_part[i * fold_rows : (i + 1) * fold_rows] for i in range(fold)], axis=1
    )

    @pl.loop(1, n)
    def _(d):
        g_copy(peer(d), me).start()

    for d in range(docs_dev):
        turned = normed_parts[d].astype(F32).T.astype(BF16)
        for j in range(n):
            feats[j % 2, j // 2 % 2, j // 4 % 2, j // 8, :, d * seq : (d + 1) * seq] = turned[
                j * rows : (j + 1) * rows
            ]
    feats_copy.start()

    def acts_start(c):
        gate_pre = pre[0, c]
        sig = jax.nn.sigmoid(gate_pre)
        acts[0, 2 * c] = (mask * pre[1, c] * sig * (1.0 + gate_pre * (1.0 - sig))).astype(BF16)
        acts[0, 2 * c + 1] = (mask * (gate_pre * sig)).astype(BF16)
        acts_copy(2 * c).start()
        acts_copy(2 * c + 1).start()

    first = nz
    early = (nz + first + 1) // 2

    @pl.loop(0, early)
    def _(c):
        acts_start(c)

    scale = own_inv / p_pair[0, :, model : model + 1] + jnp.zeros((docs_dev, 128 - down_rows), F32)
    for j in range(n):
        h_send[j // 2, j % 2, :, :down_rows] = h_own[:, j * down_rows : (j + 1) * down_rows]
        h_send[j // 2, j % 2, :, down_rows:] = scale
    h_recv[chip, core] = h_send[chip]
    lo_all[chip, core] = pack(own_unit - own_unit.astype(BF16).astype(F32))

    @pl.loop(1, chips)
    def _(d):
        h_copy(chip_peer(d), chip).start()
        lo_copy(chip_peer(d), chip).start()

    pair[...] = jnp.ones(pair.shape, F32)
    pair[:docs_dev] = p_pair[0]
    p_copy.wait_recv()
    pair[docs_dev : 2 * docs_dev] = p_pair[1]
    pooled = pair[:, :model]
    inv_norm = lax.rsqrt(jnp.sum(pooled * pooled, axis=1, keepdims=True) + EPS)
    unit_rows = pooled * inv_norm
    inv_count = inv_norm / pair[:, model : model + 1]

    e_bytes.wait_recv()
    embed = unpack(e_all[...])
    gram_student = rows_product(embed, embed)

    g_bytes.wait_recv()
    folded = jnp.sum(g_all[...], axis=0)
    gram_raw = jnp.concatenate(
        [folded[:, i * docs : (i + 1) * docs] for i in range(fold)], axis=0
    )
    diagonal = lax.broadcasted_iota(jnp.int32, (docs, docs), 0) == lax.broadcasted_iota(
        jnp.int32, (docs, docs), 1
    )
    squares = jnp.where(diagonal, gram_raw, 0.0)
    inv_col = lax.rsqrt(jnp.sum(squares, axis=1, keepdims=True) + EPS)
    inv_row = lax.rsqrt(jnp.sum(squares, axis=0, keepdims=True) + EPS)
    gram_teacher = gram_raw * inv_col * inv_row
    gram_diff = gram_student - gram_teacher

    def total(square):
        return jnp.sum(jnp.sum(square, axis=1, keepdims=True), axis=0, keepdims=True)

    diff_norm = jnp.sqrt(total(gram_diff * gram_diff) + EPS)
    teacher_norm = jnp.sqrt(total(gram_teacher * gram_teacher))
    loss_out[...] = diff_norm / teacher_norm
    d_gram = LOSS_SCALE * gram_diff / (diff_norm * teacher_norm)
    doc_at = lax.broadcasted_iota(jnp.int32, (docs, docs), 0)
    chosen = [
        jnp.sum(jnp.where(doc_at == owner * docs_dev + d, d_gram, 0.0), axis=0, keepdims=True)
        for owner in (me, sibling)
        for d in range(docs_dev)
    ]
    chosen.append(jnp.zeros((16 - 2 * docs_dev, docs), F32))
    spread = jnp.dot(
        jnp.concatenate(split3(jnp.concatenate(chosen, axis=0)), axis=0), embed,
        preferred_element_type=F32,
    )
    d_embed = 2.0 * (spread[:16] + (spread[16:32] + spread[32:]))
    along = jnp.sum(unit_rows * d_embed, axis=1, keepdims=True)
    d_wide = (d_embed - unit_rows * along) * inv_count
    d_pair = d_wide.astype(BF16)
    d_pair_hidden = rows_product(d_pair, w_down[...])
    for c in range(chunks):
        at = (c // 2) * width
        d_hid[c] = d_pair_hidden[:, at : at + width]

    feats_copy.wait_recv()

    def y_copy(c):
        return remote(y_send.at[c], y_recv.at[c], ssem.at[1], y_rsem.at[c], across)

    def y_part_copy(c, j):
        return remote(
            y_send.at[c + nn, lax.rem(j, 2), lax.div(j, 2)],
            y_recv.at[c + nn, lax.rem(j, 2), lax.div(j, 2)],
            ssem.at[1], ys_rsem.at[c, j], across,
        )

    def n_copy(c):
        return remote(n_send.at[c], n_recv.at[c], ssem.at[2], n_rsem.at[c], beside)

    def z_copy(c, there, src):
        return remote(
            z_send.at[c, there], z_recv.at[c, src], ssem.at[3], z_rsem.at[c],
            (there * 2 + parity) * 4 + lane,
        )

    def d_copy(c, there, src):
        return remote(
            d_send.at[c, there], d_recv.at[c, src], ssem.at[4], d_rsem.at[c], there * 4 + lane
        )

    def zn_copy(c):
        return remote(zn_send.at[c], zn_recv.at[c], ssem.at[5], zn_rsem.at[c], beside)

    def zz_copy(c, there, src):
        return remote(
            zz_send.at[c, :, there], zz_recv.at[c, src], ssem.at[6], zz_rsem.at[c],
            (there * 2 + parity) * 4 + lane,
        )

    def zy_copy(c):
        return remote(zy_send.at[c], zy_recv.at[c], ssem.at[7], zy_rsem.at[c], across)

    def d_acts(c):
        acts_copy(c).wait_recv()
        scaled_acts = []
        for side in range(2):
            for d in range(docs_dev):
                scale = d_hid[c, side * docs_dev + d : side * docs_dev + d + 1]
                part = acts[side, c, d * seq : (d + 1) * seq].astype(F32) * scale
                scaled_acts.append(part.astype(BF16))
        return jnp.concatenate(scaled_acts, axis=0)

    def product(own, given, right):
        left = jnp.concatenate([own.reshape(-1, tokens), given.reshape(-1, tokens)], axis=1)
        both = jnp.dot(left, right, preferred_element_type=F32)
        return both.reshape(2, halves, rows, width)

    def put(c, value):
        at = pl.ds(pl.multiple_of(lax.div(c, 2) * width, width), width)
        wide_out[lax.rem(c, 2), :, at] = value

    def z_start(c):
        right = d_acts(c)
        zn_send[c] = product(
            feats[core, :, 1 - parity], feats_in[:, 1 - parity], right
        ).astype(BF16)
        zn_copy(c).start()
        zn_part[c] = product(feats[core, :, parity], feats_in[:, parity], right)

    def zn_done(c):
        zn_copy(c).wait_recv()
        whole = zn_part[c] + zn_recv[c].astype(F32)
        zz_send[c] = whole.astype(BF16)
        zz_part[c] = zn_part[c, :, half] + zn_recv[c, :, half].astype(F32)

        @pl.loop(1, halves)
        def _(d):
            zz_copy(c, half_peer(d), half).start()

    def zz_done(c):
        window = pl.ds(0, halves - 1)
        remote(
            zz_recv.at[c, window], zz_recv.at[c, window], ssem.at[6], zz_rsem.at[c], beside
        ).wait_recv()

        @pl.loop(1, halves)
        def _(d):
            zz_part[c] += zz_recv[c, half_peer(d)].astype(F32)

        zy_send[c] = zz_part[c, 1 - row].astype(BF16)
        zy_copy(c).start()

    def y_start(c):
        right = d_acts(c + nz)
        y_send[c] = product(feats[core, 1 - row], feats_in[1 - row], right).astype(BF16)

        @pl.when(c < nn)
        def _():
            y_copy(c).start()

        @pl.when(c >= nn)
        def _():
            @pl.loop(0, cols - 1)
            def _(i):
                y_part_copy(c - nn, col_peer(far_first(i, cols))).start()

            y_part_copy(c - nn, col).start()

        y_part[c] = product(feats[core, row], feats_in[row], right)

    def n_start(c):
        y_copy(c).wait_recv()
        y_part[c] += y_recv[c].astype(F32)
        n_send[c] = y_part[c, 1 - parity].astype(BF16)
        n_copy(c).start()

    def across_sum(c, j):
        y_part_copy(c, j).wait_recv()
        at = (c + nn, lax.rem(j, 2), lax.div(j, 2))
        return y_part[at] + y_recv[at].astype(F32)

    def d_start(c):
        @pl.loop(0, cols - 1)
        def _(i):
            there = col_peer(far_first(i, cols))
            d_send[c, there] = across_sum(c, there).astype(BF16)
            d_copy(c, there, col).start()

        d_part[c] = across_sum(c, col)

    def n_done(c):
        n_copy(c).wait_recv()
        z_send[c] = (y_part[c, parity] + n_recv[c].astype(F32)).astype(BF16)
        z_part[c] = y_part[c, parity, half] + n_recv[c, half].astype(F32)

        @pl.loop(1, halves)
        def _(d):
            z_copy(c, half_peer(d), half).start()

    def within(i, count, run):
        @pl.when(jnp.logical_and(i >= 0, i < count))
        def _():
            run(i)


    def z_done(c):
        window = pl.ds(0, halves - 1)
        remote(
            z_recv.at[c, window], z_recv.at[c, window], ssem.at[3], z_rsem.at[c], beside
        ).wait_recv()

        @pl.loop(1, halves)
        def _(d):
            z_part[c] += z_recv[c, half_peer(d)].astype(F32)

        put(c + nz, z_part[c])

    def advance(c):
        within(c, ny, y_start)
        within(c, nz, z_start)
        step = c - lag
        within(step, nz, zn_done)
        within(step, nn, n_start)
        within(step - nn, nd, d_start)
        within(step - n_lag, nn, n_done)
        within(c - ny, nz, zz_done)
        within(step - z_lag, nn, z_done)

    @pl.loop(0, first)
    def _(c):
        y_start(c)
        within(c, nz, z_start)

    @pl.loop(early, pieces)
    def _(c):
        acts_start(c)

    @pl.loop(first, lag)
    def _(c):
        y_start(c)

    h_bytes.wait_recv()
    h_given.start()
    lo_bytes.wait_recv()
    lo_given.start()

    @pl.loop(lag, ny)
    def _(c):
        advance(c)

    h_given.wait_recv()
    for j in range(n):
        big_h[j * docs_dev : (j + 1) * docs_dev, :] = h_recv[j // 2, j % 2, core]
    sums = jnp.concatenate(split3(big_h[...]), axis=0)
    select = (
        lax.broadcasted_iota(jnp.int32, (down_rows, 128), 0)
        == lax.broadcasted_iota(jnp.int32, (down_rows, 128), 1)
    ).astype(F32).astype(BF16)
    own_sums = rows_product(select, sums).astype(BF16)
    lo_given.wait_recv()
    units = embed.astype(F32) + unpack(lo_all[...]).astype(F32)
    spread = jnp.dot(
        jnp.concatenate(split3(d_gram), axis=0), embed, preferred_element_type=F32
    )
    d_embed = 2.0 * (spread[:docs] + (spread[docs : 2 * docs] + spread[2 * docs :]))
    along = jnp.sum(units * d_embed, axis=1, keepdims=True)
    d_all = ((d_embed - units * along) * big_h[:, down_rows : down_rows + 1]).astype(BF16)
    down_out[...] = jnp.dot(
        own_sums, jnp.concatenate([d_all] * 3, axis=0), preferred_element_type=F32
    )

    @pl.loop(ny, ny + lag)
    def _(c):
        advance(c)

    @pl.loop(ny - n_lag, nn)
    def _(c):
        n_done(c)

    @pl.loop(lag, nz)
    def _(c):
        zz_done(c)

    @pl.loop(ny - z_lag, nn)
    def _(c):
        z_done(c)

    @pl.loop(0, nz)
    def _(c):
        zy_copy(c).wait_recv()
        put(c, zz_part[c, row] + zy_recv[c].astype(F32))

    @pl.loop(0, nd)
    def _(c):
        window = pl.ds(0, cols - 1)
        remote(
            d_recv.at[c, window], d_recv.at[c, window], ssem.at[4], d_rsem.at[c], beside
        ).wait_recv()
        z_part[nn] = d_part[c]

        @pl.loop(1, cols)
        def _(d):
            z_part[nn] += d_recv[c, col_peer(d)].astype(F32)

        put(c + nz + nn, z_part[nn])

    feats_copy.wait_send()
    t_bytes.wait_send()
    e_bytes.wait_send()
    lo_bytes.wait_send()
    h_given.wait_send()
    lo_given.wait_send()
    t_sum.wait_send()
    p_copy.wait_send()
    g_bytes.wait_send()
    h_bytes.wait_send()
    some = pl.ds(0, halves - 1)
    far = pl.ds(0, cols - 1)
    for i, sent in enumerate((
        acts.at[0], y_send, n_send, z_send.at[:, some], d_send.at[:, far], zn_send,
        zz_send.at[:, :, some], zy_send,
    )):
        remote(sent, sent, ssem.at[i], acts_rsem.at[0], beside).wait_send()


def hand_over(wide, down, gate_out, up_out, down_out, sem):
    copies = [
        pltpu.make_async_copy(made, out, sem.at[i])
        for i, (made, out) in enumerate(
            ((wide.at[0], gate_out), (wide.at[1], up_out), (down, down_out))
        )
    ]
    for copy in copies:
        copy.start()
    for copy in copies:
        copy.wait()


def solution(mesh):
    n = mesh.shape["dp"]
    in_specs = (
        P(("groups", "dp"), None),
        P(("groups", "dp")),
        P(),
        P(),
        P(),
        P(),
        P("groups", "dp"),
        P("dp", None),
        P("groups", None),
        P(),
    )
    out_specs = (
        P("groups"),
        P(("groups", "dp"), None),
        P(("groups", "dp"), None),
        P(("groups", "dp"), None),
    )

    def per_device(
        states, lengths, norm_gain, w_gate, w_up, w_down, context, w_out, resid_stream, teacher_gain
    ):
        tokens, model = states.shape
        hidden_width = w_gate.shape[1]
        docs_dev = lengths.shape[0]
        docs = context.shape[0]
        teacher_width = w_out.shape[1]
        feat = teacher_width // n
        rows = model // n
        width = 256
        chunks = 2 * hidden_width // width
        cols = n // 4
        halves = cols // 2
        nz = 2
        nd = 2
        ny = chunks - nz
        nn = ny - nd
        fold = max(1, 128 // docs)
        packed = model + 128
        hbm = pl.BlockSpec(memory_space=pl.ANY)
        vmem = pl.BlockSpec(memory_space=pltpu.VMEM)
        sem = pltpu.SemaphoreType.DMA
        loss, *made = pl.pallas_call(
            functools.partial(step_kernel, n, width, nz, nd),
            out_shape=(
                jax.ShapeDtypeStruct((1, 1), F32),
                pltpu.VMEM((2, rows, hidden_width), F32),
                pltpu.VMEM((hidden_width // n, model), F32),
            ),
            in_specs=[hbm, pl.BlockSpec(memory_space=pltpu.SMEM), vmem] + [hbm] * 6 + [vmem],
            out_specs=(vmem,) * 3,
            scratch_shapes=[
                pltpu.VMEM((tokens, model), BF16),
                pltpu.VMEM((model, hidden_width), BF16),
                pltpu.VMEM((model, hidden_width), BF16),
                pltpu.VMEM((hidden_width, model), BF16),
                pltpu.VMEM(context.shape, BF16),
                pltpu.VMEM(w_out.shape, BF16),
                pltpu.VMEM(resid_stream.shape, BF16),
                pltpu.VMEM((2, n // 2, docs, feat), F32),
                pltpu.VMEM((n // 2, docs, feat), F32),
                pltpu.VMEM((n // 2, docs, feat), BF16),
                pltpu.VMEM((n // 2, docs, feat), BF16),
                pltpu.VMEM((n, docs // fold, docs * fold), F32),
                pltpu.VMEM((2, docs_dev, packed), F32),
                pltpu.VMEM((n, docs_dev * model // 128, 128), BF16),
                pltpu.VMEM((n // 2, 2, docs_dev * model // 128, 128), BF16),
                pltpu.VMEM((docs * model // 128, 128), F32),
                pltpu.VMEM((docs_dev, hidden_width), F32),
                pltpu.VMEM((n // 2, 2, docs_dev, 128), F32),
                pltpu.VMEM((n // 2, 2, 2, docs_dev, 128), F32),
                pltpu.VMEM((docs_dev, model), F32),
                pltpu.VMEM((16, packed), F32),
                pltpu.VMEM((docs, 128), F32),
                pltpu.VMEM((2, hidden_width // width, tokens, width), F32),
                pltpu.VMEM((2, 2, 2, halves, rows, tokens), BF16),
                pltpu.VMEM((2, 2, halves, rows, tokens), BF16),
                pltpu.VMEM((2, chunks, tokens, width), BF16),
                pltpu.VMEM((chunks, 16, width), F32),
                pltpu.VMEM((ny, 2, halves, rows, width), BF16),
                pltpu.VMEM((ny, 2, halves, rows, width), F32),
                pltpu.VMEM((ny, 2, halves, rows, width), BF16),
                pltpu.VMEM((nn, halves, rows, width), BF16),
                pltpu.VMEM((nn, halves, rows, width), BF16),
                pltpu.VMEM((nn, halves, rows, width), BF16),
                pltpu.VMEM((nn, halves, rows, width), BF16),
                pltpu.VMEM((nn + 1, rows, width), F32),
                pltpu.VMEM((nd, cols, rows, width), BF16),
                pltpu.VMEM((nd, cols, rows, width), BF16),
                pltpu.VMEM((nd, rows, width), F32),
                pltpu.VMEM((nz, 2, halves, rows, width), BF16),
                pltpu.VMEM((nz, 2, halves, rows, width), BF16),
                pltpu.VMEM((nz, 2, halves, rows, width), F32),
                pltpu.VMEM((nz, 2, halves, rows, width), BF16),
                pltpu.VMEM((nz, halves, 2, rows, width), BF16),
                pltpu.VMEM((nz, 2, rows, width), F32),
                pltpu.VMEM((nz, rows, width), BF16),
                pltpu.VMEM((nz, rows, width), BF16),
                sem((5,)), sem((2, chunks // 2)), sem((5,)), sem((5,)), sem((2,)), sem((2,)), sem((2,)), sem((2,)), sem((2,)), sem((8,)),
                sem((chunks,)), sem((nn,)), sem((nd, cols)), sem((nn,)), sem((nn,)), sem((nd,)),
                sem((nz,)), sem((nz,)), sem((nz,)),
            ],
            compiler_params=pltpu.CompilerParams(
                collective_id=0, has_side_effects=True, vmem_limit_bytes=56 * 1024 * 1024
            ),
        )(
            states, lengths, norm_gain, w_gate, w_up, w_down, context, w_out,
            resid_stream, teacher_gain,
        )
        made = [pltpu.with_memory_space_constraint(m, pltpu.VMEM) for m in made]
        made = pl.pallas_call(
            hand_over,
            out_shape=(
                jax.ShapeDtypeStruct((rows, hidden_width), F32),
                jax.ShapeDtypeStruct((rows, hidden_width), F32),
                jax.ShapeDtypeStruct((hidden_width // n, model), F32),
            ),
            in_specs=[vmem] * 2,
            out_specs=(hbm,) * 3,
            scratch_shapes=[sem((3,))],
        )(*made)
        return (loss.reshape(1), *made)

    return jax.shard_map(
        per_device, mesh=mesh, in_specs=in_specs, out_specs=out_specs, check_vma=False
    )
```

```python
import functools

import jax
import jax.numpy as jnp
from jax import lax
from jax.experimental import pallas as pl
from jax.experimental.pallas import tpu as pltpu
from jax.sharding import PartitionSpec as P

EPS = 1e-06
LOSS_SCALE = 4096.0
MESH = pl.DeviceIdType.MESH
F32 = jnp.float32
BF16 = jnp.bfloat16


def rows_product(left_rows, right_rows):
    return lax.dot_general(
        left_rows, right_rows, (((1,), (1,)), ((), ())), preferred_element_type=F32
    )


def split3(wide):
    high = wide.astype(BF16)
    rest = wide - high.astype(F32)
    middle = rest.astype(BF16)
    low = (rest - middle.astype(F32)).astype(BF16)
    return high, middle, low


def step_kernel(
    n, width, nz, nd,
    states_in, lengths, norm_gain, w_gate_in, w_up_in, w_down_in, context_in, w_out_in, resid_in, gain,
    loss_out, wide_out, down_out,
    states, w_gate, w_up, w_down, context, w_out, resid,
    t_part, t_in, t_send, t_recv, g_all, p_pair, e_all, lo_all, tall, h_own, h_send, h_recv, s_own, pair, big_h,
    pre, feats, feats_in, acts, d_hid,
    y_send, y_part, y_recv, n_send, n_recv, z_send, z_recv, z_part, d_send, d_recv, d_part,
    zn_send, zn_recv, zn_part, zz_send, zz_recv, zz_part, zy_send, zy_recv,
    in_sem, wide_sem, all_ssem, all_rsem, feats_sem, t_sem, p_sem, given_ssem, given_rsem, ssem, acts_rsem,
    y_rsem, ys_rsem, n_rsem, z_rsem, d_rsem, zn_rsem, zz_rsem, zy_rsem,
):
    me = lax.axis_index("dp")
    core = lax.rem(me, 2)
    row = lax.rem(lax.div(me, 2), 2)
    col = lax.div(me, 4)
    parity = lax.rem(col, 2)
    half = lax.div(col, 2)
    cols = n // 4
    halves = cols // 2
    lane = row * 2 + core
    sibling = me + 1 - 2 * core
    across = me + 2 - 4 * row
    beside = (col + 1 - 2 * parity) * 4 + lane
    docs_dev = lengths.shape[0]
    tokens, model = states.shape
    seq = tokens // docs_dev
    hidden_width = w_gate.shape[1]
    docs = context.shape[0]
    feat = w_out.shape[1] // n
    rows = model // n
    down_rows = hidden_width // n
    pieces = hidden_width // width
    chunks = 2 * pieces
    ny = chunks - nz
    nn = ny - nd
    lag, n_lag, z_lag = 3, 1, 4

    def peer(d):
        return lax.rem(me + d, n)

    def half_peer(d):
        return lax.rem(half + d, halves)

    def col_peer(d):
        return lax.rem(col + d, cols)

    high = half * 2 // halves

    def far_first(i, count):
        return (1 - high) * (count - 1 - i) + high * (1 + i)

    def remote(src_ref, dst_ref, send_sem, recv_sem, dst):
        return pltpu.make_async_remote_copy(
            src_ref=src_ref, dst_ref=dst_ref, send_sem=send_sem, recv_sem=recv_sem,
            device_id={"dp": dst}, device_id_type=MESH,
        )

    def load(i, src, dst):
        copy = pltpu.make_async_copy(src, dst, in_sem.at[i])
        copy.start()
        return copy

    def load_wide(c):
        at = pl.ds(pl.multiple_of(c * width, width), width)
        return (
            pltpu.make_async_copy(w_gate_in.at[:, at], w_gate.at[:, at], wide_sem.at[0, c]),
            pltpu.make_async_copy(w_up_in.at[:, at], w_up.at[:, at], wide_sem.at[1, c]),
        )

    others = pl.ds(0, n - 1)
    chip = lax.div(me, 2)
    chips = n // 2
    other_chips = pl.ds(0, chips - 1)

    def chip_peer(d):
        return lax.rem(chip + d, chips)

    def t_copy(dst, src):
        return remote(
            t_send.at[dst], t_recv.at[src], all_ssem.at[0], all_rsem.at[0], 2 * dst + core
        )

    def e_copy(dst, src):
        return remote(e_all.at[src], e_all.at[src], all_ssem.at[1], all_rsem.at[1], dst)

    def g_copy(dst, src):
        return remote(g_all.at[src], g_all.at[src], all_ssem.at[2], all_rsem.at[2], dst)

    def h_copy(dst, src):
        return remote(
            h_send.at[dst], h_recv.at[src, core], all_ssem.at[3], all_rsem.at[3], 2 * dst + core
        )

    def lo_copy(dst, src):
        return remote(
            lo_all.at[src, core], lo_all.at[src, core], all_ssem.at[4], all_rsem.at[4],
            2 * dst + core,
        )

    t_bytes = remote(
        t_send.at[other_chips], t_recv.at[other_chips], all_ssem.at[0], all_rsem.at[0], sibling
    )
    e_bytes = remote(e_all.at[others], e_all.at[others], all_ssem.at[1], all_rsem.at[1], sibling)
    g_bytes = remote(g_all.at[others], g_all.at[others], all_ssem.at[2], all_rsem.at[2], sibling)
    h_bytes = remote(
        h_send.at[other_chips], h_send.at[other_chips], all_ssem.at[3], all_rsem.at[3], sibling
    )
    lo_bytes = remote(
        lo_all.at[other_chips, 0], lo_all.at[other_chips, 0], all_ssem.at[4], all_rsem.at[4],
        sibling,
    )
    h_given = remote(
        h_recv.at[:, core, 1 - core], h_recv.at[:, core, 1 - core], given_ssem.at[0],
        given_rsem.at[0], sibling,
    )
    lo_given = remote(
        lo_all.at[:, core], lo_all.at[:, core], given_ssem.at[1], given_rsem.at[1], sibling
    )
    t_sum = remote(t_part.at[1 - core], t_in, t_sem.at[0], t_sem.at[1], sibling)
    p_copy = remote(p_pair.at[0], p_pair.at[1], p_sem.at[0], p_sem.at[1], sibling)
    spans = model // 128

    def pack(row_values):
        for k in range(spans):
            tall[pl.ds(k, docs_dev, stride=spans), :] = row_values[:, k * 128 : (k + 1) * 128]
        return tall[: docs_dev * spans].astype(BF16)

    def unpack(packed_rows):
        tall[...] = packed_rows.reshape(docs * spans, 128).astype(F32)
        return jnp.concatenate(
            [tall[pl.ds(k, docs, stride=spans), :] for k in range(spans)], axis=1
        ).astype(BF16)

    context_load = load(0, context_in, context)
    w_out_load = load(1, w_out_in, w_out)
    resid_load = load(2, resid_in, resid)
    states_load = load(3, states_in, states)
    for c in range(pieces):
        for copy in load_wide(c):
            copy.start()
    w_down_load = load(4, w_down_in, w_down)

    barrier = pltpu.get_barrier_semaphore()

    @pl.loop(1, n)
    def _(d):
        pl.semaphore_signal(barrier, inc=1, device_id={"dp": peer(d)}, device_id_type=MESH)

    context_load.wait()
    w_out_load.wait()
    resid_load.wait()
    partial = jnp.dot(context[...], w_out[...], preferred_element_type=F32)
    first = (me == 0).astype(F32)
    partial = gain[...].astype(F32).reshape(1, -1) * (partial + first * resid[...].astype(F32))
    for j in range(n):
        t_part[j % 2, j // 2] = partial[:, j * feat : (j + 1) * feat]
    pl.semaphore_wait(barrier, n - 1)
    t_sum.start()

    states_load.wait()
    normed_parts = []
    masks = []
    for d in range(docs_dev):
        x = states[d * seq : (d + 1) * seq].astype(F32)
        inv_rms = lax.rsqrt(jnp.mean(x * x, axis=1, keepdims=True) + EPS)
        normed_wide = x * inv_rms * norm_gain[...].astype(F32).reshape(1, -1)
        normed = normed_wide.astype(BF16)
        normed_parts.append(normed)
        length = lengths[d]
        mask = (lax.broadcasted_iota(jnp.int32, (seq, 1), 0) < length).astype(F32)
        masks.append(mask)
        s_own[d : d + 1] = jnp.sum(x * mask, axis=0, keepdims=True)
        p_pair[0, d : d + 1, model:] = jnp.zeros((1, 128), F32) + length.astype(F32)
    normed = jnp.concatenate(normed_parts, axis=0)
    mask = jnp.concatenate(masks, axis=0)

    feats_copy = remote(feats.at[1 - core], feats_in, feats_sem.at[0], feats_sem.at[1], sibling)

    def acts_copy(c):
        return remote(acts.at[0, c], acts.at[1, c], ssem.at[0], acts_rsem.at[c], sibling)

    def forward(c):
        at = slice(c * width, (c + 1) * width)
        gate_pre = jnp.dot(normed, w_gate[:, at], preferred_element_type=F32)
        up_pre = jnp.dot(normed, w_up[:, at], preferred_element_type=F32)
        pre[0, c] = gate_pre
        pre[1, c] = up_pre
        hidden = (gate_pre * jax.nn.sigmoid(gate_pre) * up_pre).astype(BF16).astype(F32) * mask
        for d in range(docs_dev):
            h_own[d : d + 1, at] = jnp.sum(
                hidden[d * seq : (d + 1) * seq], axis=0, keepdims=True
            )

    def wide_wait(c):
        for copy in load_wide(c):
            copy.wait()

    wide_wait(0)
    forward(0)
    t_sum.wait_recv()
    t_send[...] = (t_part[core] + t_in[...]).astype(BF16)
    t_recv[chip] = t_send[chip]

    @pl.loop(0, chips - 1)
    def _(i):
        t_copy(chip_peer(far_first(i, chips)), chip).start()

    for c in range(1, pieces):
        wide_wait(c)
    for c in range(1, pieces):
        forward(c)

    w_down_load.wait()
    own_parts = jnp.concatenate([part.astype(F32) for part in split3(h_own[...])], axis=0)
    lifted = jnp.dot(own_parts.astype(BF16), w_down[...], preferred_element_type=F32)
    lifted = lifted[:docs_dev] + (lifted[docs_dev : 2 * docs_dev] + lifted[2 * docs_dev :])
    own_pooled = (s_own[...] + lifted) / p_pair[0, :, model : model + 1]
    p_pair[0, :, :model] = own_pooled
    p_copy.start()
    own_inv = lax.rsqrt(jnp.sum(own_pooled * own_pooled, axis=1, keepdims=True) + EPS)
    own_unit = own_pooled * own_inv
    e_all[me] = pack(own_unit)

    @pl.loop(0, n - 1)
    def _(i):
        e_copy(peer(far_first(i, n)), me).start()

    t_bytes.wait_recv()
    scaled = jnp.sum(t_recv[...].astype(F32), axis=0)
    scaled_high = scaled.astype(BF16)
    scaled_low = (scaled - scaled_high.astype(F32)).astype(BF16)
    crossed = rows_product(jnp.concatenate([scaled_high, scaled_low], axis=0), scaled_high)
    gram_part = crossed[:docs] + (
        crossed[docs:] + rows_product(scaled_high, scaled_low)
    )
    fold = max(1, 128 // docs)
    fold_rows = docs // fold
    g_all[me] = jnp.concatenate(
        [gram_part[i * fold_rows : (i + 1) * fold_rows] for i in range(fold)], axis=1
    )

    @pl.loop(0, n - 1)
    def _(i):
        g_copy(peer(far_first(i, n)), me).start()

    for d in range(docs_dev):
        turned = normed_parts[d].astype(F32).T.astype(BF16)
        for j in range(n):
            feats[j % 2, j // 2 % 2, j // 4 % 2, j // 8, :, d * seq : (d + 1) * seq] = turned[
                j * rows : (j + 1) * rows
            ]
    feats_copy.start()

    def acts_start(c):
        gate_pre = pre[0, c]
        sig = jax.nn.sigmoid(gate_pre)
        acts[0, 2 * c] = (mask * pre[1, c] * sig * (1.0 + gate_pre * (1.0 - sig))).astype(BF16)
        acts[0, 2 * c + 1] = (mask * (gate_pre * sig)).astype(BF16)
        acts_copy(2 * c).start()
        acts_copy(2 * c + 1).start()

    first = nz
    early = (nz + first + 1) // 2

    @pl.loop(0, early)
    def _(c):
        acts_start(c)

    scale = own_inv / p_pair[0, :, model : model + 1] + jnp.zeros((docs_dev, 128 - down_rows), F32)
    for j in range(n):
        h_send[j // 2, j % 2, :, :down_rows] = h_own[:, j * down_rows : (j + 1) * down_rows]
        h_send[j // 2, j % 2, :, down_rows:] = scale
    h_recv[chip, core] = h_send[chip]
    lo_all[chip, core] = pack(own_unit - own_unit.astype(BF16).astype(F32))

    @pl.loop(1, chips)
    def _(d):
        h_copy(chip_peer(d), chip).start()
        lo_copy(chip_peer(d), chip).start()

    pair[...] = jnp.ones(pair.shape, F32)
    pair[:docs_dev] = p_pair[0]
    p_copy.wait_recv()
    pair[docs_dev : 2 * docs_dev] = p_pair[1]
    pooled = pair[:, :model]
    inv_norm = lax.rsqrt(jnp.sum(pooled * pooled, axis=1, keepdims=True) + EPS)
    unit_rows = pooled * inv_norm
    inv_count = inv_norm / pair[:, model : model + 1]

    e_bytes.wait_recv()
    embed = unpack(e_all[...])
    gram_student = rows_product(embed, embed)

    g_bytes.wait_recv()
    folded = jnp.sum(g_all[...], axis=0)
    gram_raw = jnp.concatenate(
        [folded[:, i * docs : (i + 1) * docs] for i in range(fold)], axis=0
    )
    diagonal = lax.broadcasted_iota(jnp.int32, (docs, docs), 0) == lax.broadcasted_iota(
        jnp.int32, (docs, docs), 1
    )
    squares = jnp.where(diagonal, gram_raw, 0.0)
    inv_col = lax.rsqrt(jnp.sum(squares, axis=1, keepdims=True) + EPS)
    inv_row = lax.rsqrt(jnp.sum(squares, axis=0, keepdims=True) + EPS)
    gram_teacher = gram_raw * inv_col * inv_row
    gram_diff = gram_student - gram_teacher

    def total(square):
        return jnp.sum(jnp.sum(square, axis=1, keepdims=True), axis=0, keepdims=True)

    diff_norm = jnp.sqrt(total(gram_diff * gram_diff) + EPS)
    teacher_norm = jnp.sqrt(total(gram_teacher * gram_teacher))
    loss_out[...] = diff_norm / teacher_norm
    d_gram = LOSS_SCALE * gram_diff / (diff_norm * teacher_norm)
    doc_at = lax.broadcasted_iota(jnp.int32, (docs, docs), 0)
    chosen = [
        jnp.sum(jnp.where(doc_at == owner * docs_dev + d, d_gram, 0.0), axis=0, keepdims=True)
        for owner in (me, sibling)
        for d in range(docs_dev)
    ]
    chosen.append(jnp.zeros((16 - 2 * docs_dev, docs), F32))
    spread = jnp.dot(
        jnp.concatenate(split3(jnp.concatenate(chosen, axis=0)), axis=0), embed,
        preferred_element_type=F32,
    )
    d_embed = 2.0 * (spread[:16] + (spread[16:32] + spread[32:]))
    along = jnp.sum(unit_rows * d_embed, axis=1, keepdims=True)
    d_wide = (d_embed - unit_rows * along) * inv_count
    d_pair = d_wide.astype(BF16)
    d_pair_hidden = rows_product(d_pair, w_down[...])
    for c in range(chunks):
        at = (c // 2) * width
        d_hid[c] = d_pair_hidden[:, at : at + width]

    feats_copy.wait_recv()

    def y_copy(c):
        return remote(y_send.at[c], y_recv.at[c], ssem.at[1], y_rsem.at[c], across)

    def y_part_copy(c, j):
        return remote(
            y_send.at[c + nn, lax.rem(j, 2), lax.div(j, 2)],
            y_recv.at[c + nn, lax.rem(j, 2), lax.div(j, 2)],
            ssem.at[1], ys_rsem.at[c, j], across,
        )

    def n_copy(c):
        return remote(n_send.at[c], n_recv.at[c], ssem.at[2], n_rsem.at[c], beside)

    def z_copy(c, there, src):
        return remote(
            z_send.at[c, there], z_recv.at[c, src], ssem.at[3], z_rsem.at[c],
            (there * 2 + parity) * 4 + lane,
        )

    def d_copy(c, there, src):
        return remote(
            d_send.at[c, there], d_recv.at[c, src], ssem.at[4], d_rsem.at[c], there * 4 + lane
        )

    def zn_copy(c):
        return remote(zn_send.at[c], zn_recv.at[c], ssem.at[5], zn_rsem.at[c], beside)

    def zz_copy(c, there, src):
        return remote(
            zz_send.at[c, :, there], zz_recv.at[c, src], ssem.at[6], zz_rsem.at[c],
            (there * 2 + parity) * 4 + lane,
        )

    def zy_copy(c):
        return remote(zy_send.at[c], zy_recv.at[c], ssem.at[7], zy_rsem.at[c], across)

    def d_acts(c):
        acts_copy(c).wait_recv()
        scaled_acts = []
        for side in range(2):
            for d in range(docs_dev):
                scale = d_hid[c, side * docs_dev + d : side * docs_dev + d + 1]
                part = acts[side, c, d * seq : (d + 1) * seq].astype(F32) * scale
                scaled_acts.append(part.astype(BF16))
        return jnp.concatenate(scaled_acts, axis=0)

    def product(own, given, right):
        left = jnp.concatenate([own.reshape(-1, tokens), given.reshape(-1, tokens)], axis=1)
        both = jnp.dot(left, right, preferred_element_type=F32)
        return both.reshape(2, halves, rows, width)

    def put(c, value):
        at = pl.ds(pl.multiple_of(lax.div(c, 2) * width, width), width)
        wide_out[lax.rem(c, 2), :, at] = value

    def z_start(c):
        right = d_acts(c)
        zn_send[c] = product(
            feats[core, :, 1 - parity], feats_in[:, 1 - parity], right
        ).astype(BF16)
        zn_copy(c).start()
        zn_part[c] = product(feats[core, :, parity], feats_in[:, parity], right)

    def zn_done(c):
        zn_copy(c).wait_recv()
        whole = zn_part[c] + zn_recv[c].astype(F32)
        zz_send[c] = whole.astype(BF16)
        zz_part[c] = zn_part[c, :, half] + zn_recv[c, :, half].astype(F32)

        @pl.loop(1, halves)
        def _(d):
            zz_copy(c, half_peer(d), half).start()

    def zz_done(c):
        window = pl.ds(0, halves - 1)
        remote(
            zz_recv.at[c, window], zz_recv.at[c, window], ssem.at[6], zz_rsem.at[c], beside
        ).wait_recv()

        @pl.loop(1, halves)
        def _(d):
            zz_part[c] += zz_recv[c, half_peer(d)].astype(F32)

        zy_send[c] = zz_part[c, 1 - row].astype(BF16)
        zy_copy(c).start()

    def y_start(c):
        right = d_acts(c + nz)
        y_send[c] = product(feats[core, 1 - row], feats_in[1 - row], right).astype(BF16)

        @pl.when(c < nn)
        def _():
            y_copy(c).start()

        @pl.when(c >= nn)
        def _():
            @pl.loop(0, cols - 1)
            def _(i):
                y_part_copy(c - nn, col_peer(far_first(i, cols))).start()

            y_part_copy(c - nn, col).start()

        y_part[c] = product(feats[core, row], feats_in[row], right)

    def n_start(c):
        y_copy(c).wait_recv()
        n_send[c] = (y_part[c, 1 - parity] + y_recv[c, 1 - parity].astype(F32)).astype(BF16)
        n_copy(c).start()
        y_part[c, parity] += y_recv[c, parity].astype(F32)

    def across_sum(c, j):
        y_part_copy(c, j).wait_recv()
        at = (c + nn, lax.rem(j, 2), lax.div(j, 2))
        return y_part[at] + y_recv[at].astype(F32)

    def d_start(c):
        @pl.loop(0, cols - 1)
        def _(i):
            there = col_peer(far_first(i, cols))
            d_send[c, there] = across_sum(c, there).astype(BF16)
            d_copy(c, there, col).start()

        d_part[c] = across_sum(c, col)

    def n_done(c):
        n_copy(c).wait_recv()
        z_send[c] = (y_part[c, parity] + n_recv[c].astype(F32)).astype(BF16)
        z_part[c] = y_part[c, parity, half] + n_recv[c, half].astype(F32)

        @pl.loop(1, halves)
        def _(d):
            z_copy(c, half_peer(d), half).start()

    def within(i, count, run):
        @pl.when(jnp.logical_and(i >= 0, i < count))
        def _():
            run(i)


    def z_done(c):
        window = pl.ds(0, halves - 1)
        remote(
            z_recv.at[c, window], z_recv.at[c, window], ssem.at[3], z_rsem.at[c], beside
        ).wait_recv()

        @pl.loop(1, halves)
        def _(d):
            z_part[c] += z_recv[c, half_peer(d)].astype(F32)

        put(c + nz, z_part[c])

    def advance(c):
        within(c, ny, y_start)
        within(c, nz, z_start)
        step = c - lag
        within(step, nz, zn_done)
        within(step, nn, n_start)
        within(step - nn, nd, d_start)
        within(step - n_lag, nn, n_done)
        within(c - ny, nz, zz_done)
        within(step - z_lag, nn, z_done)

    @pl.loop(0, first)
    def _(c):
        y_start(c)
        within(c, nz, z_start)

    @pl.loop(early, pieces)
    def _(c):
        acts_start(c)

    @pl.loop(first, lag)
    def _(c):
        y_start(c)

    h_bytes.wait_recv()
    h_given.start()
    lo_bytes.wait_recv()
    lo_given.start()

    @pl.loop(lag, ny)
    def _(c):
        advance(c)

    h_given.wait_recv()
    for j in range(n):
        big_h[j * docs_dev : (j + 1) * docs_dev, :] = h_recv[j // 2, j % 2, core]
    sums = jnp.concatenate(split3(big_h[...]), axis=0)
    select = (
        lax.broadcasted_iota(jnp.int32, (down_rows, 128), 0)
        == lax.broadcasted_iota(jnp.int32, (down_rows, 128), 1)
    ).astype(F32).astype(BF16)
    own_sums = rows_product(select, sums).astype(BF16)
    lo_given.wait_recv()
    units = embed.astype(F32) + unpack(lo_all[...]).astype(F32)
    spread = jnp.dot(
        jnp.concatenate(split3(d_gram), axis=0), embed, preferred_element_type=F32
    )
    d_embed = 2.0 * (spread[:docs] + (spread[docs : 2 * docs] + spread[2 * docs :]))
    along = jnp.sum(units * d_embed, axis=1, keepdims=True)
    d_all = ((d_embed - units * along) * big_h[:, down_rows : down_rows + 1]).astype(BF16)
    down_out[...] = jnp.dot(
        own_sums, jnp.concatenate([d_all] * 3, axis=0), preferred_element_type=F32
    )

    @pl.loop(ny, ny + lag)
    def _(c):
        advance(c)

    @pl.loop(ny - n_lag, nn)
    def _(c):
        n_done(c)

    @pl.loop(lag, nz)
    def _(c):
        zz_done(c)

    @pl.loop(ny - z_lag, nn)
    def _(c):
        z_done(c)

    @pl.loop(0, nz)
    def _(c):
        zy_copy(c).wait_recv()
        put(c, zz_part[c, row] + zy_recv[c].astype(F32))

    @pl.loop(0, nd)
    def _(c):
        window = pl.ds(0, cols - 1)
        remote(
            d_recv.at[c, window], d_recv.at[c, window], ssem.at[4], d_rsem.at[c], beside
        ).wait_recv()
        z_part[nn] = d_part[c]

        @pl.loop(1, cols)
        def _(d):
            z_part[nn] += d_recv[c, col_peer(d)].astype(F32)

        put(c + nz + nn, z_part[nn])

    feats_copy.wait_send()
    t_bytes.wait_send()
    e_bytes.wait_send()
    lo_bytes.wait_send()
    h_given.wait_send()
    lo_given.wait_send()
    t_sum.wait_send()
    p_copy.wait_send()
    g_bytes.wait_send()
    h_bytes.wait_send()
    some = pl.ds(0, halves - 1)
    far = pl.ds(0, cols - 1)
    for i, sent in enumerate((
        acts.at[0], y_send, n_send, z_send.at[:, some], d_send.at[:, far], zn_send,
        zz_send.at[:, :, some], zy_send,
    )):
        remote(sent, sent, ssem.at[i], acts_rsem.at[0], beside).wait_send()


def hand_over(wide, down, gate_out, up_out, down_out, sem):
    copies = [
        pltpu.make_async_copy(made, out, sem.at[i])
        for i, (made, out) in enumerate(
            ((wide.at[0], gate_out), (wide.at[1], up_out), (down, down_out))
        )
    ]
    for copy in copies:
        copy.start()
    for copy in copies:
        copy.wait()


def solution(mesh):
    n = mesh.shape["dp"]
    in_specs = (
        P(("groups", "dp"), None),
        P(("groups", "dp")),
        P(),
        P(),
        P(),
        P(),
        P("groups", "dp"),
        P("dp", None),
        P("groups", None),
        P(),
    )
    out_specs = (
        P("groups"),
        P(("groups", "dp"), None),
        P(("groups", "dp"), None),
        P(("groups", "dp"), None),
    )

    def per_device(
        states, lengths, norm_gain, w_gate, w_up, w_down, context, w_out, resid_stream, teacher_gain
    ):
        tokens, model = states.shape
        hidden_width = w_gate.shape[1]
        docs_dev = lengths.shape[0]
        docs = context.shape[0]
        teacher_width = w_out.shape[1]
        feat = teacher_width // n
        rows = model // n
        width = 256
        chunks = 2 * hidden_width // width
        cols = n // 4
        halves = cols // 2
        nz = 2
        nd = 2
        ny = chunks - nz
        nn = ny - nd
        fold = max(1, 128 // docs)
        packed = model + 128
        hbm = pl.BlockSpec(memory_space=pl.ANY)
        vmem = pl.BlockSpec(memory_space=pltpu.VMEM)
        sem = pltpu.SemaphoreType.DMA
        loss, *made = pl.pallas_call(
            functools.partial(step_kernel, n, width, nz, nd),
            out_shape=(
                jax.ShapeDtypeStruct((1, 1), F32),
                pltpu.VMEM((2, rows, hidden_width), F32),
                pltpu.VMEM((hidden_width // n, model), F32),
            ),
            in_specs=[hbm, pl.BlockSpec(memory_space=pltpu.SMEM), vmem] + [hbm] * 6 + [vmem],
            out_specs=(vmem,) * 3,
            scratch_shapes=[
                pltpu.VMEM((tokens, model), BF16),
                pltpu.VMEM((model, hidden_width), BF16),
                pltpu.VMEM((model, hidden_width), BF16),
                pltpu.VMEM((hidden_width, model), BF16),
                pltpu.VMEM(context.shape, BF16),
                pltpu.VMEM(w_out.shape, BF16),
                pltpu.VMEM(resid_stream.shape, BF16),
                pltpu.VMEM((2, n // 2, docs, feat), F32),
                pltpu.VMEM((n // 2, docs, feat), F32),
                pltpu.VMEM((n // 2, docs, feat), BF16),
                pltpu.VMEM((n // 2, docs, feat), BF16),
                pltpu.VMEM((n, docs // fold, docs * fold), F32),
                pltpu.VMEM((2, docs_dev, packed), F32),
                pltpu.VMEM((n, docs_dev * model // 128, 128), BF16),
                pltpu.VMEM((n // 2, 2, docs_dev * model // 128, 128), BF16),
                pltpu.VMEM((docs * model // 128, 128), F32),
                pltpu.VMEM((docs_dev, hidden_width), F32),
                pltpu.VMEM((n // 2, 2, docs_dev, 128), F32),
                pltpu.VMEM((n // 2, 2, 2, docs_dev, 128), F32),
                pltpu.VMEM((docs_dev, model), F32),
                pltpu.VMEM((16, packed), F32),
                pltpu.VMEM((docs, 128), F32),
                pltpu.VMEM((2, hidden_width // width, tokens, width), F32),
                pltpu.VMEM((2, 2, 2, halves, rows, tokens), BF16),
                pltpu.VMEM((2, 2, halves, rows, tokens), BF16),
                pltpu.VMEM((2, chunks, tokens, width), BF16),
                pltpu.VMEM((chunks, 16, width), F32),
                pltpu.VMEM((ny, 2, halves, rows, width), BF16),
                pltpu.VMEM((ny, 2, halves, rows, width), F32),
                pltpu.VMEM((ny, 2, halves, rows, width), BF16),
                pltpu.VMEM((nn, halves, rows, width), BF16),
                pltpu.VMEM((nn, halves, rows, width), BF16),
                pltpu.VMEM((nn, halves, rows, width), BF16),
                pltpu.VMEM((nn, halves, rows, width), BF16),
                pltpu.VMEM((nn + 1, rows, width), F32),
                pltpu.VMEM((nd, cols, rows, width), BF16),
                pltpu.VMEM((nd, cols, rows, width), BF16),
                pltpu.VMEM((nd, rows, width), F32),
                pltpu.VMEM((nz, 2, halves, rows, width), BF16),
                pltpu.VMEM((nz, 2, halves, rows, width), BF16),
                pltpu.VMEM((nz, 2, halves, rows, width), F32),
                pltpu.VMEM((nz, 2, halves, rows, width), BF16),
                pltpu.VMEM((nz, halves, 2, rows, width), BF16),
                pltpu.VMEM((nz, 2, rows, width), F32),
                pltpu.VMEM((nz, rows, width), BF16),
                pltpu.VMEM((nz, rows, width), BF16),
                sem((5,)), sem((2, chunks // 2)), sem((5,)), sem((5,)), sem((2,)), sem((2,)), sem((2,)), sem((2,)), sem((2,)), sem((8,)),
                sem((chunks,)), sem((nn,)), sem((nd, cols)), sem((nn,)), sem((nn,)), sem((nd,)),
                sem((nz,)), sem((nz,)), sem((nz,)),
            ],
            compiler_params=pltpu.CompilerParams(
                collective_id=0, has_side_effects=True, vmem_limit_bytes=56 * 1024 * 1024
            ),
        )(
            states, lengths, norm_gain, w_gate, w_up, w_down, context, w_out,
            resid_stream, teacher_gain,
        )
        made = [pltpu.with_memory_space_constraint(m, pltpu.VMEM) for m in made]
        made = pl.pallas_call(
            hand_over,
            out_shape=(
                jax.ShapeDtypeStruct((rows, hidden_width), F32),
                jax.ShapeDtypeStruct((rows, hidden_width), F32),
                jax.ShapeDtypeStruct((hidden_width // n, model), F32),
            ),
            in_specs=[vmem] * 2,
            out_specs=(hbm,) * 3,
            scratch_shapes=[sem((3,))],
        )(*made)
        return (loss.reshape(1), *made)

    return jax.shard_map(
        per_device, mesh=mesh, in_specs=in_specs, out_specs=out_specs, check_vma=False
    )
```
